256 devices in a mesh: cfg: 2 (over x_lo), wide: 32 (over x_hi, z, core), narrow: 4 (over y).
Axes of the slice: x: 4 (x_hi: 2, x_lo: 2; x = x_hi * 2 + x_lo), y: 4, z: 8, core: 2. Of those that a mesh axis runs over, the one named last changes fastest.
Arguments:
- hidden: bfloat16 [2, 4096, 3072], P('cfg', 'wide', 'narrow'), may hold values from -120 to 120
- split_table: int32 [32], replicated, may hold values from 1 to 128, 2048 in all
- modulation: float32 [8, 3072], P(None, 'narrow'), may hold values from -4 to 4
- expand_weight: bfloat16 [3072, 12288], P('narrow', 'wide'), may hold values from -0.109375 to 0.109375
- contract_weight: bfloat16 [12288, 3072], P('wide', 'narrow'), may hold values from -0.0546875 to 0.0546875
- output_weight: bfloat16 [3072, 64], P('narrow'), may hold values from -0.109375 to 0.109375
- latent: float32 [4096, 64], P('wide'), may hold values from -6 to 6
- timestep: int32 [1], replicated, may hold values from 20 to 499
Outputs:
- layer_out: bfloat16 [2, 4096, 3072], P('cfg', 'wide', 'narrow')
- clean_latent: float32 [4096, 64], P('wide')
The draws below stay inside these ranges and needn't reach their ends.
Inputs may be any that keep to these rules, and one draw needn't show every extreme that they name: `split_table`: the entries sum to 2048, and the largest is exactly 128.
All inputs are finite; a program needn't handle non-finite values.
Results may differ from the reference program's by a relative error of at most 0.0056.
Values may be sent and summed in bfloat16 or wider, within the bound.
A program may use at most 64 MiB of HBM per device.

```python
import math
import jax
import jax.numpy as jnp
import numpy as np
from jax import lax

D = 3072
FF = 12288
PATCH = 64
TEXT = 226
CAP = 128
SLOTS = 4096
TOKENS = 2048
N_WIDE = 32


def draw_hidden(key, part):
    keys = jax.random.split(key, 4)
    column = jnp.arange(D, dtype=jnp.float32) / (D - 1)
    jitter = jax.random.uniform(keys[1], (D,), jnp.float32, 0.7, 1.3)
    row_draw = jax.random.uniform(keys[2], (2, SLOTS, 1), jnp.float32, 0.0, 1.0)
    centre = jnp.clip(jax.random.normal(keys[3], (2, SLOTS, 1), jnp.float32), -3.0, 3.0)
    base = jnp.clip(jax.random.normal(keys[0], (2, SLOTS, D), jnp.float32), -4.0, 4.0)
    column_scale = 3.0 ** column * jitter
    row_scale = 10.0 ** row_draw
    return (0.3 * row_scale * (base * column_scale + centre)).astype(jnp.bfloat16)


def steps_of(rng, dims, pieces, least, top_value):
    factor_of = 1.0
    for dim, parts in pieces:
        heights = jax.random.uniform(jax.random.fold_in(jax.random.fold_in(rng, 6), dim), (parts,), jnp.float32, least / len(pieces), top_value / len(pieces))
        factor_of = factor_of * jnp.repeat(jnp.exp(heights), dims[dim] // parts).reshape((-1,) + (1,) * (len(dims) - 1 - dim))
    return factor_of


def split_up(number_of, total, bound, lean):
    loads = [(1 << 20) // math.isqrt(grade ** lean) + 1 for grade in range(2, number_of + 1)]
    rest, counts = total - bound - (number_of - 1), [1] * (number_of - 1)
    while rest > 0:
        movable = [i for i in range(number_of - 1) if counts[i] < bound]
        whole, remaining = sum([loads[i] for i in movable]), rest
        for i in movable:
            more = min(bound - counts[i], max(1, remaining * loads[i] // whole), rest)
            counts[i] = counts[i] + more
            rest = rest - more
    return np.array([bound] + counts)


def uneven_parts(rng, count, total, reach, skew):
    if count == 2:
        one = jax.random.randint(rng, (), max(1, total - reach), min(reach, total - 1) + 1)
        return jnp.stack([one, total - one])
    sizes = jnp.asarray(split_up(count, total, reach, skew), jnp.int32)
    couples = (count - 1) // 2
    source_of, taker = sizes[1:1 + 2 * couples:2], sizes[2:2 + 2 * couples:2]
    room = jnp.minimum(source_of - 1, reach - taker)
    shifted = jax.random.randint(jax.random.fold_in(rng, 1), (couples,), 0, 1 << 20) % (room + 1)
    sizes = sizes.at[1:1 + 2 * couples:2].set(source_of - shifted).at[2:2 + 2 * couples:2].set(taker + shifted)
    return sizes[jax.random.permutation(jax.random.fold_in(rng, 2), count)]


def normal_values(stream_key, shape, spread, most, pieces=(), held_as=jnp.bfloat16):
    values = spread * jax.random.normal(stream_key, shape, jnp.float32)
    if pieces:
        values = values * steps_of(stream_key, shape, pieces, -0.22, 0.18)
    return jnp.clip(values, -most, most).astype(held_as)


def setup_inputs(seed: int = 0) -> dict:
    key_of = jax.random.split(jax.random.key(seed), 9)
    return {
        "hidden": draw_hidden(jax.random.fold_in(key_of[8], 71), 0),
        "split_table": uneven_parts(key_of[1], N_WIDE, TOKENS, CAP, 1).astype(jnp.int32),
        "modulation": normal_values(key_of[2], (8, D), 1.0, 4.0, ((1, 4),), jnp.float32),
        "expand_weight": normal_values(key_of[3], (D, FF), D ** -0.5, 0.109375, ((0, 4), (1, 32))),
        "contract_weight": normal_values(key_of[4], (FF, D), FF ** -0.5, 0.0546875, ((0, 32), (1, 4))),
        "output_weight": normal_values(key_of[5], (D, PATCH), D ** -0.5, 0.109375, ((0, 4),)),
        "latent": normal_values(key_of[6], (SLOTS, PATCH), 1.0, 6.0, ((0, 32),), jnp.float32),
        "timestep": jax.random.randint(key_of[7], (1,), 20, 500).astype(jnp.int32),
    }


norm_eps = 1e-05
guidance = 6.0

def alpha_table():
    steps_index = jnp.arange(1000, dtype=jnp.int32)
    start_root = 0.00085 ** 0.5
    end_root = 0.012 ** 0.5
    roots = start_root + (end_root - start_root) * steps_index.astype(jnp.float32) / 999.0
    return (steps_index, jnp.cumprod(1.0 - roots * roots))

def layer_norm(values, shifts, scaling):
    average = lax.optimization_barrier(jnp.sum(values, -1, keepdims=True)) / D
    squares = lax.optimization_barrier(jnp.sum(values * values, -1, keepdims=True)) / D
    variance = squares - average * average
    return (values - average) * lax.rsqrt(variance + norm_eps) * (1.0 + scaling) + shifts

def reference(hidden, split_table, modulation, expand_weight, contract_weight, output_weight, latent, timestep):
    slot_total = N_WIDE * CAP
    slot_index = jnp.arange(slot_total, dtype=jnp.int32)
    block_index = slot_index // CAP
    inner_index = slot_index % CAP
    offsets = jnp.cumsum(split_table) - split_table
    position = offsets[block_index] + inner_index
    slot_live = inner_index < split_table[block_index]
    is_text = slot_live & (position < TEXT)
    is_video = slot_live & (position >= TEXT)
    text_column = is_text[:, None]
    shifts = jnp.where(text_column, modulation[3], modulation[0])
    scaling = jnp.where(text_column, modulation[4], modulation[1])
    gating = jnp.where(text_column, modulation[5], modulation[2])
    values = hidden.astype(jnp.float32)
    normed = layer_norm(values, shifts, scaling).astype(jnp.bfloat16)

    def feed_forward(row_block):
        hidden_pre = jnp.dot(row_block, expand_weight, preferred_element_type=jnp.float32)
        activated = jax.nn.gelu(hidden_pre, approximate=True).astype(jnp.bfloat16)
        return jnp.dot(activated, contract_weight, preferred_element_type=jnp.float32)
    ff_result = lax.map(feed_forward, normed.reshape(2 * N_WIDE, CAP, D)).reshape(2, slot_total, D)
    layer_out = jnp.where(slot_live[:, None], values + gating * ff_result, 0.0).astype(jnp.bfloat16)
    final_in = layer_out.astype(jnp.float32)
    final_normed = layer_norm(final_in, modulation[6], modulation[7]).astype(jnp.bfloat16)
    velocity_cond = jnp.dot(final_normed[0], output_weight, preferred_element_type=jnp.float32)
    velocity_uncond = jnp.dot(final_normed[1], output_weight, preferred_element_type=jnp.float32)
    guided = guidance * velocity_cond + (1.0 - guidance) * velocity_uncond
    steps_index, alpha_bar = alpha_table()
    alpha_now = jnp.sum(jnp.where(steps_index == timestep[0], alpha_bar, 0.0))
    clean_latent = jnp.where(is_video[:, None], jnp.sqrt(alpha_now) * latent - jnp.sqrt(1.0 - alpha_now) * guided, 0.0)
    return (layer_out, clean_latent)
```

```python
import functools

import jax
import jax.numpy as jnp
import numpy as np
from jax import lax
from jax.experimental import pallas as pl
from jax.experimental.pallas import tpu as pltpu
from jax.sharding import PartitionSpec as P

TEXT = 226
EPS = 1e-05
GUIDANCE = 6.0
MESH = pl.DeviceIdType.MESH
F32 = jnp.float32
BF16 = jnp.bfloat16


def alpha_table():
    start_root = 0.00085**0.5
    end_root = 0.012**0.5
    roots = start_root + (end_root - start_root) * np.arange(1000) / 999.0
    table = np.zeros((8, 128), np.float32)
    table.reshape(-1)[:1000] = np.cumprod(1.0 - roots * roots)
    return table


def body(
    sizes,
    split_ref,
    time_ref,
    hidden_ref,
    mod_ref,
    w1_ref,
    w2_ref,
    ow_ref,
    latent_ref,
    alpha_ref,
    out_ref,
    clean_ref,
    xr,
    modg,
    owg,
    w1g,
    w2g,
    nst,
    xa,
    hid,
    act,
    sib_s,
    sib_r,
    ring_s,
    ring_r,
    tot,
    xs,
    xv,
    fs,
    fr,
    ffb,
    lo,
    vel_s,
    vel_r,
    cl,
    y_s,
    y_r,
    w_s,
    w_r,
    loc,
    ag_s,
    ag_r,
    sb_s,
    sb_r,
    x_s,
    x_r,
    i_s,
    i_r,
    pr_s,
    pr_r,
    rg_s,
    rg_r,
    c_s,
    c_r,
    o_s,
    o_r,
):
    nz, ny, q, bl, ff, feats = sizes
    half = 2 * q
    cfg = lax.axis_index("cfg")
    w = lax.axis_index("wide")
    n = lax.axis_index("narrow")
    core = lax.rem(w, 2)
    z = lax.rem(w // 2, nz)
    xh = w // (2 * nz)
    d = 1 - 2 * core

    def wide_of(xh_, z_, core_):
        return xh_ * (2 * nz) + z_ * 2 + core_

    def zmod(v):
        return lax.rem(v + 2 * nz, nz)

    def yid(k):
        return lax.rem(n + k, ny)

    sib = (cfg, wide_of(xh, z, 1 - core), n)
    xpart = (cfg, wide_of(1 - xh, z, core), n)
    znext = (cfg, wide_of(xh, zmod(z + d), core), n)
    zprev = (cfg, wide_of(xh, zmod(z - d), core), n)
    cpart = (1 - cfg, w, n)

    def ypeer(k):
        return (cfg, w, yid(k))

    def rcopy(src, dst, ssem, rsem, dev):
        return pltpu.make_async_remote_copy(
            src_ref=src, dst_ref=dst, send_sem=ssem, recv_sem=rsem, device_id=dev, device_id_type=MESH
        )

    def arrived(dst, rsem):
        rcopy(dst, dst, rsem, rsem, sib).wait_recv()

    def sent(src, ssem):
        rcopy(src, src, ssem, ssem, sib).wait_send()

    barrier = pltpu.get_barrier_semaphore()
    partners = [ypeer(1), ypeer(2), ypeer(3), sib, xpart, znext, zprev, cpart]
    for dev in partners:
        pl.semaphore_signal(barrier, inc=1, device_id=dev, device_id_type=MESH)
    pl.semaphore_wait(barrier, len(partners))

    def rows_of(i, size):
        return pl.ds(pl.multiple_of(i * size, size), size)

    for k in (1, 3, 2):
        m = yid(k)
        rcopy(hidden_ref.at[rows_of(m, q), :], xr.at[n], y_s.at[0, k - 1], y_r.at[0, k - 1], ypeer(k)).start()
    for k in (1, 3, 2):
        rcopy(mod_ref, modg.at[n], y_s.at[1, k - 1], y_r.at[1, k - 1], ypeer(k)).start()
    own = [
        (hidden_ref.at[rows_of(n, q), :], xr.at[n]),
        (mod_ref, modg.at[n]),
        (ow_ref, owg.at[n]),
        (w1_ref, w1g.at[n]),
        (w2_ref, w2g.at[n]),
    ]
    for i, (src, dst) in enumerate(own):
        pltpu.make_async_copy(src, dst, loc.at[i]).start()
    weights = [(w1_ref, w1g, bl // 2), (w2_ref, w2g, ff // 2)]

    def weight_out(i):
        src, dst, _ = weights[i]
        rcopy(src, dst.at[n], w_s.at[i, 0], w_r.at[i, 0], ypeer(1)).start()
        rcopy(src, dst.at[n], w_s.at[i, 1], w_r.at[i, 1], ypeer(3)).start()

    def weight_on(i):
        _, dst, part = weights[i]
        arrived(dst.at[yid(3)], w_r.at[i, 0])
        first = dst.at[yid(3), pl.ds(0, part), :]
        rcopy(first, first, w_s.at[i, 2], w_r.at[i, 2], ypeer(1)).start()
        arrived(dst.at[yid(1)], w_r.at[i, 1])
        second = dst.at[yid(1), pl.ds(part, part), :]
        rcopy(second, second, w_s.at[i, 3], w_r.at[i, 3], ypeer(3)).start()

    def weight_in(i):
        _, dst, part = weights[i]
        arrived(dst.at[yid(2), pl.ds(0, part), :], w_r.at[i, 2])
        arrived(dst.at[yid(2), pl.ds(part, part), :], w_r.at[i, 3])

    weight_out(0)
    for k in (1, 3, 2):
        rcopy(ow_ref, owg.at[n], y_s.at[2, k - 1], y_r.at[2, k - 1], ypeer(k)).start()

    offset = jnp.int32(0)
    count = jnp.int32(0)
    for b in range(split_ref.shape[0]):
        value = split_ref[b]
        offset = offset + jnp.where(b < w, value, 0)
        count = count + jnp.where(b == w, value, 0)
    slot = n * q + lax.broadcasted_iota(jnp.int32, (q, 1), 0)
    live = slot < count
    text = live & (slot + offset < TEXT)
    video = live & (slot + offset >= TEXT)

    def pick(b, row_text, row_video):
        return jnp.where(text, modg[b, pl.ds(row_text, 1), :], modg[b, pl.ds(row_video, 1), :])

    def stats(total, squares):
        average = total / feats
        variance = squares / feats - average * average
        return average, lax.rsqrt(variance + EPS)

    pltpu.make_async_copy(own[0][0], own[0][1], loc.at[0]).wait()
    pltpu.make_async_copy(own[1][0], own[1][1], loc.at[1]).wait()
    for k in (1, 2, 3):
        arrived(xr.at[yid(ny - k)], y_r.at[0, k - 1])
    total = jnp.zeros((q, 1), F32)
    squares = jnp.zeros((q, 1), F32)
    for b in range(ny):
        v = xr[b].astype(F32)
        total = total + jnp.sum(v, -1, keepdims=True)
        squares = squares + jnp.sum(v * v, -1, keepdims=True)
    average, scale = stats(total, squares)
    for k in (1, 2, 3):
        arrived(modg.at[yid(ny - k)], y_r.at[1, k - 1])
    for b in range(ny):
        v = xr[b].astype(F32)
        nst[b] = ((v - average) * scale * (1.0 + pick(b, 4, 1)) + pick(b, 3, 0)).astype(BF16)

    mine = 2 * core
    other = 2 * (1 - core)
    own_rows = rows_of(xh * 2 + core, q)
    sib_rows = rows_of(xh * 2 + 1 - core, q)
    a_rows = rows_of(xh, half)
    b_rows = rows_of(1 - xh, half)

    rcopy(
        nst.at[pl.ds(other, 2)], xa.at[z, pl.ds(other, 2), own_rows, :], i_s.at[0], i_r.at[0], sib
    ).start()
    for j in range(2):
        xa[z, mine + j, own_rows, :] = nst[mine + j]
    arrived(xa.at[z, pl.ds(mine, 2), sib_rows, :], i_r.at[0])

    def ag(o, rows):
        return xa.at[o, pl.ds(mine, 2), rows, :]

    def side(o, first):
        return xa.at[o, pl.ds(first, 2), :, :]

    rcopy(ag(z, a_rows), ag(z, a_rows), x_s.at[0], x_r.at[0], xpart).start()
    hid[...] = jnp.zeros_like(hid)

    def work(i, carry):
        o = zmod(z - d * i)
        hid[o] = hid[o] + (
            jnp.dot(xa[o, mine], w1g[mine], preferred_element_type=F32)
            + jnp.dot(xa[o, mine + 1], w1g[mine + 1], preferred_element_type=F32)
        )
        p = zmod(z + d * i)
        arrived(side(p, other), sb_r.at[i])
        hid[p] = hid[p] + (
            jnp.dot(xa[p, other], w1g[other], preferred_element_type=F32)
            + jnp.dot(xa[p, other + 1], w1g[other + 1], preferred_element_type=F32)
        )
        return carry

    def gelu(o):
        v = hid[o]
        act[o] = (0.5 * v * (1.0 + jnp.tanh(0.7978845608 * (v + 0.044715 * (v * v * v))))).astype(BF16)

    ready = min(3, nz - 2)
    done_work = 0
    for s in range(nz):
        o = zmod(z - d * s)
        last = s == nz - 1
        if s > 0:
            arrived(ag(o, a_rows), ag_r.at[s - 1, 0])
        if not last:
            rcopy(ag(o, a_rows), ag(o, a_rows), ag_s.at[s, 0], ag_r.at[s, 0], znext).start()
        if s == 0:
            arrived(ag(z, b_rows), x_r.at[0])
        else:
            arrived(ag(o, b_rows), ag_r.at[s - 1, 1])
        if not last:
            rcopy(ag(o, b_rows), ag(o, b_rows), ag_s.at[s, 1], ag_r.at[s, 1], znext).start()
        rcopy(side(o, mine), side(o, mine), sb_s.at[s], sb_r.at[s], sib).start()
        if s == min(2, nz - 2):
            pltpu.make_async_copy(own[3][0], own[3][1], loc.at[3]).wait()
            weight_on(0)
            weight_out(1)
        if s == ready:
            weight_in(0)
        if s >= ready:
            upto = nz if last else min(s, 2 * (s - ready) + 2)
            lax.fori_loop(done_work, upto, work, 0)
            done_work = upto
        if s == min(5, nz - 2):
            pltpu.make_async_copy(own[4][0], own[4][1], loc.at[4]).wait()
            weight_on(1)

    lax.fori_loop(0, nz, lambda i, carry: (gelu(i), carry)[1], 0)
    weight_in(1)

    def sib_part(s):
        p = zmod(z + d * (1 + s))
        for j in range(2):
            sib_s[s, j] = jnp.dot(act[p], w2g[other + j], preferred_element_type=F32).astype(BF16)
        rcopy(sib_s.at[s], sib_r.at[s], pr_s.at[s], pr_r.at[s], sib).start()

    def own_part(s, j):
        p = zmod(z - d * (1 + s))
        return jnp.dot(act[p], w2g[mine + j], preferred_element_type=F32)

    def ring_out(s, j):
        rcopy(ring_s.at[s, j], ring_r.at[s, j], rg_s.at[s, j], rg_r.at[s, j], znext).start()

    sib_part(0)
    sib_part(1)
    arrived(sib_r.at[0], pr_r.at[0])
    for j in range(2):
        ring_s[0, j] = (own_part(0, j) + sib_r[0, j].astype(F32)).astype(BF16)
        ring_out(0, j)

    def ring_step(s, carry):
        sib_part(s + 1)
        arrived(sib_r.at[s], pr_r.at[s])
        for j in range(2):
            part = own_part(s, j) + sib_r[s, j].astype(F32)
            arrived(ring_r.at[s - 1, j], rg_r.at[s - 1, j])
            ring_s[s, j] = (part + ring_r[s - 1, j].astype(F32)).astype(BF16)
            ring_out(s, j)
        return carry

    lax.fori_loop(1, nz - 1, ring_step, 0)
    end = nz - 1
    arrived(sib_r.at[end], pr_r.at[end])
    for j in range(2):
        tot[j] = own_part(end, j) + sib_r[end, j].astype(F32)
        arrived(ring_r.at[end - 1, j], rg_r.at[end - 1, j])
        tot[j] = tot[j] + ring_r[end - 1, j].astype(F32)
        xs[j] = tot[j, b_rows, :].astype(BF16)
        rcopy(xs.at[j], xv.at[j], x_s.at[1 + j], x_r.at[1 + j], xpart).start()
    for j in range(2):
        arrived(xv.at[j], x_r.at[1 + j])
        fs[j] = (tot[j, sib_rows, :] + xv[j, rows_of(1 - core, q), :].astype(F32)).astype(BF16)
    rcopy(fs, fr, i_s.at[1], i_r.at[1], sib).start()
    for j in range(2):
        ffb[mine + j] = tot[j, own_rows, :] + xv[j, rows_of(core, q), :].astype(F32)
    arrived(fr, i_r.at[1])
    for j in range(2):
        ffb[other + j] = fr[j].astype(F32)

    total = jnp.zeros((q, 1), F32)
    squares = jnp.zeros((q, 1), F32)
    for b in range(ny):
        v = xr[b].astype(F32) + pick(b, 5, 2) * ffb[b]
        v = jnp.where(live, v, 0.0).astype(BF16)
        lo[b] = v
        v = v.astype(F32)
        total = total + jnp.sum(v, -1, keepdims=True)
        squares = squares + jnp.sum(v * v, -1, keepdims=True)
    out_rows = rows_of(n, q)
    for k in (1, 3, 2):
        rcopy(lo.at[yid(k)], out_ref.at[out_rows, :], o_s.at[0, k - 1], o_r.at[0, k - 1], ypeer(k)).start()
    pltpu.make_async_copy(lo.at[n], out_ref.at[out_rows, :], loc.at[5]).start()
    average, scale = stats(total, squares)
    pltpu.make_async_copy(own[2][0], own[2][1], loc.at[2]).wait()
    for k in (1, 2, 3):
        arrived(owg.at[yid(ny - k)], y_r.at[2, k - 1])
    velocity = jnp.zeros((q, ow_ref.shape[1]), F32)
    for b in range(ny):
        v = (lo[b].astype(F32) - average) * scale
        v = (v * (1.0 + modg[b, pl.ds(7, 1), :]) + modg[b, pl.ds(6, 1), :]).astype(BF16)
        velocity = velocity + jnp.dot(v, owg[b], preferred_element_type=F32)
    vel_s[...] = velocity * jnp.where(cfg == 0, GUIDANCE, 1.0 - GUIDANCE)
    rcopy(vel_s, vel_r, c_s.at[0], c_r.at[0], cpart).start()
    index = lax.broadcasted_iota(jnp.int32, (8, 128), 0) * 128 + lax.broadcasted_iota(jnp.int32, (8, 128), 1)
    alpha = jnp.where(index == time_ref[0], alpha_ref[...], 0.0)
    alpha = jnp.sum(jnp.sum(alpha, 0, keepdims=True), 1, keepdims=True)
    scaled = jnp.sqrt(alpha) * latent_ref[out_rows, :]
    arrived(vel_r, c_r.at[0])
    guided = vel_s[...] + vel_r[...]
    cl[...] = jnp.where(video, scaled - jnp.sqrt(1.0 - alpha) * guided, 0.0)
    for k in (1, 3, 2):
        rcopy(cl, clean_ref.at[out_rows, :], o_s.at[1, k - 1], o_r.at[1, k - 1], ypeer(k)).start()
    pltpu.make_async_copy(cl, clean_ref.at[out_rows, :], loc.at[6]).start()

    for k in (1, 2, 3):
        sent(hidden_ref.at[rows_of(yid(k), q), :], y_s.at[0, k - 1])
        sent(mod_ref, y_s.at[1, k - 1])
        sent(ow_ref, y_s.at[2, k - 1])
    for i, (src, dst, part) in enumerate(weights):
        sent(src, w_s.at[i, 0])
        sent(src, w_s.at[i, 1])
        sent(dst.at[yid(3), pl.ds(0, part), :], w_s.at[i, 2])
        sent(dst.at[yid(1), pl.ds(part, part), :], w_s.at[i, 3])
    sent(nst.at[pl.ds(other, 2)], i_s.at[0])
    sent(ag(z, a_rows), x_s.at[0])
    for s in range(nz):
        o = zmod(z - d * s)
        if s < nz - 1:
            sent(ag(o, a_rows), ag_s.at[s, 0])
            sent(ag(o, b_rows), ag_s.at[s, 1])
            for j in range(2):
                sent(ring_s.at[s, j], rg_s.at[s, j])
        sent(side(o, mine), sb_s.at[s])
        sent(sib_s.at[s], pr_s.at[s])
    for j in range(2):
        sent(xs.at[j], x_s.at[1 + j])
    sent(fs, i_s.at[1])
    sent(vel_s, c_s.at[0])
    for k in (1, 2, 3):
        sent(lo.at[yid(k)], o_s.at[0, k - 1])
        sent(cl, o_s.at[1, k - 1])
        arrived(out_ref.at[rows_of(yid(ny - k), q), :], o_r.at[0, k - 1])
        arrived(clean_ref.at[rows_of(yid(ny - k), q), :], o_r.at[1, k - 1])
    pltpu.make_async_copy(lo.at[n], out_ref.at[out_rows, :], loc.at[5]).wait()
    pltpu.make_async_copy(cl, clean_ref.at[out_rows, :], loc.at[6]).wait()


def on_device(n_wide, n_narrow, hidden, split_table, modulation, w1, w2, ow, latent, timestep):
    cap, bl = hidden.shape[1:]
    ff = w1.shape[1]
    patch = ow.shape[1]
    ny = n_narrow
    nz = n_wide // 4
    q = cap // ny
    rows = 4 * q
    sizes = (nz, ny, q, bl, ff, bl * ny)
    dma = pltpu.SemaphoreType.DMA
    vm = pltpu.VMEM
    scratch = [
        vm((ny, q, bl), BF16),
        vm((ny, 8, bl), F32),
        vm((ny, bl, patch), BF16),
        vm((ny, bl, ff), BF16),
        vm((ny, ff, bl), BF16),
        vm((ny, q, bl), BF16),
        vm((nz, ny, rows, bl), BF16),
        vm((nz, rows, ff), F32),
        vm((nz, rows, ff), BF16),
        vm((nz, 2, rows, bl), BF16),
        vm((nz, 2, rows, bl), BF16),
        vm((nz - 1, 2, rows, bl), BF16),
        vm((nz - 1, 2, rows, bl), BF16),
        vm((2, rows, bl), F32),
        vm((2, 2 * q, bl), BF16),
        vm((2, 2 * q, bl), BF16),
        vm((2, q, bl), BF16),
        vm((2, q, bl), BF16),
        vm((ny, q, bl), F32),
        vm((ny, q, bl), BF16),
        vm((q, patch), F32),
        vm((q, patch), F32),
        vm((q, patch), F32),
        dma((3, 3)),
        dma((3, 3)),
        dma((2, 4)),
        dma((2, 4)),
        dma((7,)),
        dma((nz - 1, 2)),
        dma((nz - 1, 2)),
        dma((nz,)),
        dma((nz,)),
        dma((3,)),
        dma((3,)),
        dma((2,)),
        dma((2,)),
        dma((nz,)),
        dma((nz,)),
        dma((nz - 1, 2)),
        dma((nz - 1, 2)),
        dma((1,)),
        dma((1,)),
        dma((2, 3)),
        dma((2, 3)),
    ]
    anyspec = pl.BlockSpec(memory_space=pl.ANY)
    smem = pl.BlockSpec(memory_space=pltpu.SMEM)
    vmem = pl.BlockSpec(memory_space=pltpu.VMEM)
    layer_out, clean = pl.pallas_call(
        functools.partial(body, sizes),
        out_shape=(
            jax.ShapeDtypeStruct((cap, bl), BF16),
            jax.ShapeDtypeStruct((cap, patch), F32),
        ),
        in_specs=[smem, smem, anyspec, anyspec, anyspec, anyspec, anyspec, vmem, vmem],
        out_specs=(anyspec, anyspec),
        scratch_shapes=scratch,
        compiler_params=pltpu.CompilerParams(
            collective_id=0, has_side_effects=True, vmem_limit_bytes=48 * 1024 * 1024
        ),
    )(
        split_table,
        timestep,
        hidden[0],
        modulation,
        w1,
        w2,
        ow,
        latent,
        jnp.asarray(alpha_table()),
    )
    return (layer_out[None], clean)


def solution(mesh):
    return jax.shard_map(
        functools.partial(on_device, mesh.shape["wide"], mesh.shape["narrow"]),
        mesh=mesh,
        in_specs=(
            P("cfg", "wide", "narrow"),
            P(),
            P(None, "narrow"),
            P("narrow", "wide"),
            P("wide", "narrow"),
            P("narrow", None),
            P("wide", None),
            P(),
        ),
        out_specs=(P("cfg", "wide", "narrow"), P("wide", None)),
        check_vma=False,
    )
```

```python
import functools

import jax
import jax.numpy as jnp
import numpy as np
from jax import lax
from jax.experimental import pallas as pl
from jax.experimental.pallas import tpu as pltpu
from jax.sharding import PartitionSpec as P

TEXT = 226
EPS = 1e-05
GUIDANCE = 6.0
MESH = pl.DeviceIdType.MESH
F32 = jnp.float32
BF16 = jnp.bfloat16
I32 = jnp.int32


def alpha_table():
    start_root = 0.00085**0.5
    end_root = 0.012**0.5
    roots = start_root + (end_root - start_root) * np.arange(1000) / 999.0
    table = np.zeros((8, 128), np.float32)
    table.reshape(-1)[:1000] = np.cumprod(1.0 - roots * roots)
    return table


def dot(a, b):
    return jnp.dot(a, b, preferred_element_type=F32)


def dot_nt(a, b):
    return lax.dot_general(a, b, (((1,), (1,)), ((), ())), preferred_element_type=F32)


def iota(shape, dim):
    return lax.broadcasted_iota(I32, shape, dim)


def one_hot(condition):
    return jnp.where(condition, 1.0, 0.0).astype(BF16)


def body(
    sizes,
    split_ref,
    time_ref,
    hidden_ref,
    latent_ref,
    alpha_ref,
    mod_ref,
    w1_ref,
    w2_ref,
    ow_ref,
    out_ref,
    clean_ref,
    slab_s,
    slab_r,
    xr,
    modg,
    owg,
    w1g,
    w2g,
    nst,
    gx,
    spread,
    xa,
    hid,
    act,
    sib_s,
    sib_r,
    ring_s,
    ring_r,
    tot,
    es,
    er,
    ffb,
    lo,
    back_s,
    back_r,
    vel_s,
    vel_r,
    a_s,
    a_r,
    b_s,
    b_r,
    y_s,
    y_r,
    w_s,
    w_r,
    loc,
    e_s,
    e_r,
    ag_s,
    ag_r,
    sb_s,
    sb_r,
    pr_s,
    pr_r,
    rg_s,
    rg_r,
    f_s,
    f_r,
    c_s,
    c_r,
):
    nz, ny, q, gr, bl, ff, cap, patch = sizes
    feats = ny * bl
    hb = bl // 2
    groups = ny * nz
    la, lb = nz // 2, nz - 1 - nz // 2
    cfg = lax.axis_index("cfg")
    w = lax.axis_index("wide")
    n = lax.axis_index("narrow")
    core = lax.rem(w, 2)
    z = lax.rem(w // 2, nz)
    xh = w // (2 * nz)
    d = 1 - 2 * core

    def wide_of(xh_, z_, core_):
        return xh_ * (2 * nz) + z_ * 2 + core_

    def zmod(v):
        return lax.rem(v + 2 * nz, nz)

    def yid(k):
        return lax.rem(n + k, ny)

    sib = (cfg, wide_of(xh, z, 1 - core), n)
    xpart = (cfg, wide_of(1 - xh, z, core), n)
    diag = (cfg, wide_of(1 - xh, z, 1 - core), n)
    znext = (cfg, wide_of(xh, zmod(z + d), core), n)
    zprev = (cfg, wide_of(xh, zmod(z - d), core), n)
    cpart = (1 - cfg, w, n)

    def ypeer(k):
        return (cfg, w, yid(k))

    def peer(k):
        m = lax.rem(n + k // nz, ny)
        zd = lax.rem(z + lax.rem(k, nz), nz)
        return m * nz + zd, (cfg, wide_of(xh, zd, core), m)

    def source(k):
        m = lax.rem(n + ny - k // nz, ny)
        zd = lax.rem(z + nz - lax.rem(k, nz), nz)
        return m * nz + zd

    def rcopy(src, dst, ssem, rsem, dev):
        return pltpu.make_async_remote_copy(
            src_ref=src, dst_ref=dst, send_sem=ssem, recv_sem=rsem, device_id=dev, device_id_type=MESH
        )

    def arrived(dst, rsem):
        rcopy(dst, dst, rsem, rsem, sib).wait_recv()

    def sent(src, ssem):
        rcopy(src, src, ssem, ssem, sib).wait_send()

    def signal(dev):
        pl.semaphore_signal(barrier, inc=1, device_id=dev, device_id_type=MESH)

    def times(count, action, first=0):
        def step(k, carry):
            action(k)
            return carry

        lax.fori_loop(first, count, step, 0)

    barrier = pltpu.get_barrier_semaphore()
    times(groups, lambda k: signal(peer(k)[1]), 1)
    for dev in (sib, xpart, diag, cpart):
        signal(dev)

    own = [(mod_ref, modg.at[n]), (w1_ref, w1g.at[n]), (w2_ref, w2g.at[n]), (ow_ref, owg.at[n])]
    for i, (src, dst) in enumerate(own):
        pltpu.make_async_copy(src, dst, loc.at[i]).start()

    def rows_of(i, size):
        return pl.ds(pl.multiple_of(i * size, size), size)

    offset = jnp.int32(0)
    count = jnp.int32(0)
    for b in range(split_ref.shape[0]):
        value = split_ref[b]
        offset = offset + jnp.where(b < w, value, 0)
        count = count + jnp.where(b == w, value, 0)
    row = iota((groups * 8, cap), 0)
    residue = (row >> 3) * 4 + (row & 3)
    hit = residue == ((iota((groups * 8, cap), 1) + offset) & (cap - 1))
    low = (row & 4) == 0
    slabs = dot(one_hot(hit & low), hidden_ref[:, :hb]) + dot(one_hot(hit & ~low), hidden_ref[:, hb:])
    slab_s[...] = slabs.reshape(groups, 8, hb).astype(BF16)
    pl.semaphore_wait(barrier, groups - 1 + 4)

    def slab_out(k):
        target, dev = peer(k)
        rcopy(slab_s.at[target], slab_r.at[n * nz + z], a_s.at[k - 1], a_r.at[k - 1], dev).start()

    times(groups, slab_out, 1)
    for k in (1, 3, 2):
        rcopy(mod_ref, modg.at[n], y_s.at[0, k - 1], y_r.at[0, k - 1], ypeer(k)).start()
    slab_r[n * nz + z] = slab_s[n * nz + z]
    weights = [(w1_ref, w1g, bl // 2), (w2_ref, w2g, ff // 2)]

    def weight_out(i):
        src, dst, _ = weights[i]
        rcopy(src, dst.at[n], w_s.at[i, 0], w_r.at[i, 0], ypeer(1)).start()
        rcopy(src, dst.at[n], w_s.at[i, 1], w_r.at[i, 1], ypeer(3)).start()

    def weight_on(i):
        _, dst, part = weights[i]
        pltpu.make_async_copy(own[1 + i][0], own[1 + i][1], loc.at[1 + i]).wait()
        arrived(dst.at[yid(3)], w_r.at[i, 0])
        first = dst.at[yid(3), pl.ds(0, part), :]
        rcopy(first, first, w_s.at[i, 2], w_r.at[i, 2], ypeer(1)).start()
        arrived(dst.at[yid(1)], w_r.at[i, 1])
        second = dst.at[yid(1), pl.ds(part, part), :]
        rcopy(second, second, w_s.at[i, 3], w_r.at[i, 3], ypeer(3)).start()

    def weight_in(i):
        _, dst, part = weights[i]
        arrived(dst.at[yid(2), pl.ds(0, part), :], w_r.at[i, 2])
        arrived(dst.at[yid(2), pl.ds(part, part), :], w_r.at[i, 3])

    weight_out(0)
    for k in (1, 3, 2):
        rcopy(ow_ref, owg.at[n], y_s.at[1, k - 1], y_r.at[1, k - 1], ypeer(k)).start()
    hid[...] = jnp.zeros_like(hid)

    def slot_table(shape, dim):
        index = iota(shape, dim)
        member = index // q
        inner = index - member * q
        block = (member >> 1) * (2 * nz) + (inner >> 2) * 2 + (member & 1)
        off = jnp.zeros(shape, I32)
        cnt = jnp.zeros(shape, I32)
        for b in range(split_ref.shape[0]):
            value = split_ref[b]
            off = off + jnp.where(block > b, value, 0)
            cnt = cnt + jnp.where(block == b, value, 0)
        lane = inner & 3
        inside = ((n * nz + z) * 4 + lane - off) & (cap - 1)
        position = off + inside
        live = inside < cnt
        spot = jnp.where(live, lane * (gr // 4) + position // cap, -1)
        return live, position, spot

    lane_spot = slot_table((1, 4 * q), 1)[2]
    compact = one_hot(iota((gr, 4 * q), 0) == lane_spot)
    row_live, row_position, row_spot = slot_table((4 * q, 1), 0)
    spread[...] = jnp.where(iota((4 * q, gr), 1) == row_spot, 1.0, 0.0)
    member = xh * 2 + core
    state = jnp.where(row_live, jnp.where(row_position < TEXT, 2, 1), 0)
    tables = jnp.zeros((q, 1), I32)
    for i in range(4):
        tables = tables + jnp.where(member == i, state[i * q : (i + 1) * q], 0)
    live = tables > 0
    text = tables == 2

    def pick(b, row_text, row_video):
        return jnp.where(text, modg[b, pl.ds(row_text, 1), :], modg[b, pl.ds(row_video, 1), :])

    def stats(total, squares):
        average = total / feats
        variance = squares / feats - average * average
        return average, lax.rsqrt(variance + EPS)

    unrow = iota((q, 2 * q), 0)
    uncol = iota((q, 2 * q), 1)
    unhit = ((unrow >> 2) == (uncol >> 3)) & ((unrow & 3) == (uncol & 3))
    unlow = (uncol & 4) == 0
    take_low = one_hot(unhit & unlow)
    take_high = one_hot(unhit & ~unlow)
    times(groups, lambda k: arrived(slab_r.at[source(k)], a_r.at[k - 1]), 1)
    total = jnp.zeros((q, 1), F32)
    squares = jnp.zeros((q, 1), F32)
    for b in range(ny):
        v = slab_r[b * nz : (b + 1) * nz].astype(F32).reshape(nz * 8, hb).astype(BF16)
        for part, take in ((0, take_low), (1, take_high)):
            u = dot(take, v)
            xr[b, :, part * hb : (part + 1) * hb] = u.astype(BF16)
            total = total + jnp.sum(u, -1, keepdims=True)
            squares = squares + jnp.sum(u * u, -1, keepdims=True)
    average, scale = stats(total, squares)
    pltpu.make_async_copy(own[0][0], own[0][1], loc.at[0]).wait()
    for k in (1, 2, 3):
        arrived(modg.at[yid(ny - k)], y_r.at[0, k - 1])
    for b in range(ny):
        v = xr[b].astype(F32)
        nst[b] = ((v - average) * scale * (1.0 + pick(b, 4, 1)) + pick(b, 3, 0)).astype(BF16)

    mine = 2 * core
    other = 2 * (1 - core)
    own_rows = rows_of(member, q)
    mates = [(sib, xh * 2 + 1 - core, other), (xpart, (1 - xh) * 2 + core, mine), (diag, (1 - xh) * 2 + 1 - core, other)]
    for i in (1, 2, 0):
        dev, _, blk = mates[i]
        rcopy(nst.at[pl.ds(blk, 2)], gx.at[:, own_rows, :], e_s.at[i], e_r.at[i], dev).start()
    for j in range(2):
        gx[j, own_rows, :] = nst[mine + j]
    for i in range(3):
        arrived(gx.at[:, rows_of(mates[i][1], q), :], e_r.at[i])
    for j in range(2):
        xa[z, mine + j] = dot(compact, gx[j]).astype(BF16)

    def side(o, first):
        return xa.at[o, pl.ds(first, 2)]

    def relay(o, j, sem, dev):
        rcopy(xa.at[o, mine + j], xa.at[o, mine + j], ag_s.at[sem, j], ag_r.at[sem, j], dev).start()

    def share(u):
        o = zmod(z + d * u)
        rcopy(side(o, mine), side(o, mine), sb_s.at[u % nz], sb_r.at[u % nz], sib).start()

    def work(u):
        o = zmod(z + d * u)
        hid[o] = hid[o] + (dot(xa[o, mine], w1g[mine]) + dot(xa[o, mine + 1], w1g[mine + 1]))
        p = zmod(z - d * u)
        arrived(side(p, other), sb_r.at[zmod(u)])
        hid[p] = hid[p] + (dot(xa[p, other], w1g[other]) + dot(xa[p, other + 1], w1g[other + 1]))

    def gelu(o):
        v = hid[o]
        act[o] = (0.5 * v * (1.0 + jnp.tanh(0.7978845608 * (v + 0.044715 * (v * v * v))))).astype(BF16)

    for s in range(la):
        for j in range(2):
            if s > 0:
                arrived(xa.at[zmod(z - d * s), mine + j], ag_r.at[s - 1, j])
            relay(zmod(z - d * s), j, s, znext)
            if 0 < s <= lb:
                arrived(xa.at[zmod(z + d * s), mine + j], ag_r.at[la + s - 1, j])
            if s < lb:
                relay(zmod(z + d * s), j, la + s, zprev)
        share(-s)
        if 0 < s <= lb:
            share(s)
        if s == min(1, la - 1):
            weight_on(0)
            weight_out(1)
        if s == la - 1:
            weight_in(0)
            work(0)

            def pair(k):
                work(k)
                work(-k)

            times(la, pair, 1)
    for j in range(2):
        arrived(xa.at[zmod(z - d * la), mine + j], ag_r.at[la - 1, j])
    share(-la)
    for s in range(la, lb + 1):
        for j in range(2):
            arrived(xa.at[zmod(z + d * s), mine + j], ag_r.at[la + s - 1, j])
        share(s)
    weight_on(1)
    for u in range(la, nz - la + 1):
        work(u)
    times(nz, gelu)

    far = lax.rem(n + 2, ny)

    def blk_of(side_, b):
        near = side_ == n // 2
        first = jnp.where(near, n, far + 1 - 2 * lax.rem(far, 2))
        second = jnp.where(near, n + 1 - 2 * lax.rem(n, 2), far)
        return first if b == 0 else second

    order = []
    for s in range(la):
        order.append(("next", s, la - s))
        if s < lb:
            order.append(("prev", s, -(lb - s)))
    order.append(("stay", 0, 0))
    slot_of = {(kind, s): t for t, (kind, s, _) in enumerate(order)}

    def sib_part(t, b):
        p = zmod(z - d * order[t][2])
        sib_s[t, b] = dot(act[p], w2g[blk_of(1 - core, b)]).astype(BF16)
        rcopy(sib_s.at[t, b], sib_r.at[t, b], pr_s.at[t, b], pr_r.at[t, b], sib).start()

    def ring_part(t, b):
        kind, s, u = order[t]
        part = dot(act[zmod(z + d * u)], w2g[blk_of(core, b)])
        arrived(sib_r.at[t, b], pr_r.at[t, b])
        part = part + sib_r[t, b].astype(F32)
        if kind == "stay":
            before = [slot_of[("next", la - 1)]] + ([slot_of[("prev", lb - 1)]] if lb else [])
        else:
            before = [slot_of[(kind, s - 1)]] if s else []
        for p in before:
            arrived(ring_r.at[p, b], rg_r.at[p, b])
            part = part + ring_r[p, b].astype(F32)
        if kind == "stay":
            tot[b] = part.astype(BF16)
            for i in range(3):
                dev, index, _ = mates[i]
                es[i, b] = dot(spread[rows_of(index, q), :].astype(BF16), tot[b]).astype(BF16)
                rcopy(es.at[i, b], er.at[i, b], f_s.at[i, b], f_r.at[i, b], dev).start()
            return
        ring_s[t, b] = part.astype(BF16)
        rcopy(
            ring_s.at[t, b], ring_r.at[t, b], rg_s.at[t, b], rg_r.at[t, b], znext if kind == "next" else zprev
        ).start()

    stages = {}
    for t, (kind, s, _) in enumerate(order):
        stages.setdefault(la if kind == "stay" else s, []).append(t)
    lag = 2
    events = []
    for step in range(la + 1 + lag):
        for b in range(2):
            at = step - lag * b
            if 0 <= at <= la:
                events += [(t, b) for t in stages[at]]
    ahead = 2
    for t, b in events[:ahead]:
        sib_part(t, b)
    needs_far = False
    for i, (t, b) in enumerate(events):
        if i + ahead < len(events):
            if events[i + ahead][1] == 1 and not needs_far:
                weight_in(1)
                needs_far = True
            sib_part(*events[i + ahead])
        ring_part(t, b)

    for b in range(2):
        arrived(er.at[1, b], f_r.at[1, b])
        ffb[blk_of(core, b)] = dot(spread[own_rows, :].astype(BF16), tot[b]) + er[1, b].astype(F32)
    for b in range(2):
        arrived(er.at[0, b], f_r.at[0, b])
        arrived(er.at[2, b], f_r.at[2, b])
        ffb[blk_of(1 - core, b)] = er[0, b].astype(F32) + er[2, b].astype(F32)
    total = jnp.zeros((q, 1), F32)
    squares = jnp.zeros((q, 1), F32)
    for b in range(ny):
        v = xr[b].astype(F32) + pick(b, 5, 2) * ffb[b]
        v = jnp.where(live, v, 0.0).astype(BF16)
        lo[b] = v
        v = v.astype(F32)
        total = total + jnp.sum(v, -1, keepdims=True)
        squares = squares + jnp.sum(v * v, -1, keepdims=True)
    average, scale = stats(total, squares)
    pltpu.make_async_copy(own[3][0], own[3][1], loc.at[3]).wait()
    for k in (1, 2, 3):
        arrived(owg.at[yid(ny - k)], y_r.at[1, k - 1])
    velocity = jnp.zeros((q, patch), F32)
    for b in range(ny):
        v = (lo[b].astype(F32) - average) * scale
        v = (v * (1.0 + modg[b, pl.ds(7, 1), :]) + modg[b, pl.ds(6, 1), :]).astype(BF16)
        velocity = velocity + dot_nt(v, owg[b])
    velocity = velocity * jnp.where(cfg == 0, GUIDANCE, 1.0 - GUIDANCE)

    coarse = velocity.astype(BF16)
    fine = (velocity - coarse.astype(F32)).astype(BF16)
    backrow = iota((2 * q, q), 0)
    backcol = iota((2 * q, q), 1)
    backhit = ((backcol >> 2) == (backrow >> 3)) & ((backcol & 3) == (backrow & 3))
    backlow = (backrow & 4) == 0
    put_low = one_hot(backhit & backlow)
    put_high = one_hot(backhit & ~backlow)
    terms = dot(put_low, jnp.concatenate([coarse, fine], axis=1)).reshape(nz, 8, 2 * patch).astype(BF16)
    for b in range(ny):
        v = dot(put_low, lo[b, :, :hb]) + dot(put_high, lo[b, :, hb:])
        back_s[b * nz : (b + 1) * nz, :, :hb] = v.reshape(nz, 8, hb).astype(BF16)
        back_s[b * nz : (b + 1) * nz, :, hb:] = terms

    def back_out(k):
        target, dev = peer(k)
        rcopy(back_s.at[target], back_r.at[n * nz + z], b_s.at[k - 1], b_r.at[k - 1], dev).start()

    times(groups, back_out, 1)
    back_r[n * nz + z] = back_s[n * nz + z]

    column = iota((cap, groups * 8), 1)
    undo = ((column >> 3) * 4 + (column & 3)) == ((iota((cap, groups * 8), 0) + offset) & (cap - 1))
    undo_low = one_hot(undo & ((column & 4) == 0))
    undo_high = one_hot(undo & ((column & 4) != 0))
    index = iota((8, 128), 0) * 128 + iota((8, 128), 1)
    alpha = jnp.where(index == time_ref[0], alpha_ref[...], 0.0)
    alpha = jnp.sum(jnp.sum(alpha, 0, keepdims=True), 1, keepdims=True)
    scaled = jnp.sqrt(alpha) * latent_ref[...]
    factor = jnp.sqrt(1.0 - alpha)
    lanes = iota((1, cap), 1)
    video = (lanes < count) & (lanes + offset >= TEXT)
    times(groups, lambda k: arrived(back_r.at[source(k)], b_r.at[k - 1]), 1)
    v = back_r[:, :, hb:].astype(F32).reshape(groups * 8, 2 * patch).astype(BF16)
    v = dot(undo_low, v).T
    vel_s[...] = v[:patch] + v[patch:]
    rcopy(vel_s, vel_r, c_s.at[0], c_r.at[0], cpart).start()
    v = back_r[:, :, :hb].astype(F32).reshape(groups * 8, hb).astype(BF16)
    out_ref[:, :hb] = dot(undo_low, v).astype(BF16)
    out_ref[:, hb:] = dot(undo_high, v).astype(BF16)

    def slabs_sent(k):
        target = peer(k)[0]
        sent(slab_s.at[target], a_s.at[k - 1])
        sent(back_s.at[target], b_s.at[k - 1])

    times(groups, slabs_sent, 1)
    for k in (1, 2, 3):
        sent(mod_ref, y_s.at[0, k - 1])
        sent(ow_ref, y_s.at[1, k - 1])
    for i, (src, dst, part) in enumerate(weights):
        sent(src, w_s.at[i, 0])
        sent(src, w_s.at[i, 1])
        sent(dst.at[yid(3), pl.ds(0, part), :], w_s.at[i, 2])
        sent(dst.at[yid(1), pl.ds(part, part), :], w_s.at[i, 3])
    for i in range(3):
        sent(nst.at[pl.ds(mates[i][2], 2)], e_s.at[i])
        for b in range(2):
            sent(es.at[i, b], f_s.at[i, b])
    for s in range(la):
        for j in range(2):
            sent(xa.at[zmod(z - d * s), mine + j], ag_s.at[s, j])
    for s in range(lb):
        for j in range(2):
            sent(xa.at[zmod(z + d * s), mine + j], ag_s.at[la + s, j])
    for t in range(nz):
        sent(side(zmod(z + d * t), mine), sb_s.at[t])
        for b in range(2):
            sent(sib_s.at[t, b], pr_s.at[t, b])
            if t < nz - 1:
                sent(ring_s.at[t, b], rg_s.at[t, b])
    arrived(vel_r, c_r.at[0])
    clean_ref[...] = jnp.where(video, scaled - factor * (vel_s[...] + vel_r[...]), 0.0)
    sent(vel_s, c_s.at[0])


def on_device(n_wide, n_narrow, hidden, split_table, modulation, w1, w2, ow, latent, timestep):
    cap, bl = hidden.shape[1:]
    ff = w1.shape[1]
    patch = ow.shape[1]
    ny = n_narrow
    nz = n_wide // 4
    q = cap // ny
    gr = n_wide * 2
    sizes = (nz, ny, q, gr, bl, ff, cap, patch)
    groups = ny * nz
    hb = bl // 2
    dma = pltpu.SemaphoreType.DMA
    vm = pltpu.VMEM
    scratch = [
        vm((groups, 8, hb), BF16),
        vm((groups, 8, hb), BF16),
        vm((ny, q, bl), BF16),
        vm((ny, 8, bl), F32),
        vm((ny, patch, bl), BF16),
        vm((ny, bl, ff), BF16),
        vm((ny, ff, bl), BF16),
        vm((ny, q, bl), BF16),
        vm((2, 4 * q, bl), BF16),
        vm((4 * q, gr), F32),
        vm((nz, ny, gr, bl), BF16),
        vm((nz, gr, ff), F32),
        vm((nz, gr, ff), BF16),
        vm((nz, 2, gr, bl), BF16),
        vm((nz, 2, gr, bl), BF16),
        vm((nz - 1, 2, gr, bl), BF16),
        vm((nz - 1, 2, gr, bl), BF16),
        vm((2, gr, bl), BF16),
        vm((3, 2, q, bl), BF16),
        vm((3, 2, q, bl), BF16),
        vm((ny, q, bl), F32),
        vm((ny, q, bl), BF16),
        vm((groups, 8, hb + 2 * patch), BF16),
        vm((groups, 8, hb + 2 * patch), BF16),
        vm((patch, cap), F32),
        vm((patch, cap), F32),
        dma((groups - 1,)),
        dma((groups - 1,)),
        dma((groups - 1,)),
        dma((groups - 1,)),
        dma((2, 3)),
        dma((2, 3)),
        dma((2, 4)),
        dma((2, 4)),
        dma((4,)),
        dma((3,)),
        dma((3,)),
        dma((nz - 1, 2)),
        dma((nz - 1, 2)),
        dma((nz,)),
        dma((nz,)),
        dma((nz, 2)),
        dma((nz, 2)),
        dma((nz - 1, 2)),
        dma((nz - 1, 2)),
        dma((3, 2)),
        dma((3, 2)),
        dma((1,)),
        dma((1,)),
    ]
    hbm = pl.BlockSpec(memory_space=pltpu.HBM)
    smem = pl.BlockSpec(memory_space=pltpu.SMEM)
    vmem = pl.BlockSpec(memory_space=pltpu.VMEM)
    layer_out, clean = pl.pallas_call(
        functools.partial(body, sizes),
        out_shape=(
            jax.ShapeDtypeStruct((cap, bl), BF16),
            jax.ShapeDtypeStruct((patch, cap), F32),
        ),
        in_specs=[smem, smem, vmem, vmem, vmem, hbm, hbm, hbm, hbm],
        out_specs=(vmem, vmem),
        scratch_shapes=scratch,
        compiler_params=pltpu.CompilerParams(
            collective_id=0, has_side_effects=True, vmem_limit_bytes=48 * 1024 * 1024
        ),
    )(
        split_table,
        timestep,
        hidden[0],
        latent.T,
        jnp.asarray(alpha_table()),
        modulation,
        w1,
        w2,
        ow.T,
    )
    return (layer_out[None], clean.T)


def solution(mesh):
    return jax.shard_map(
        functools.partial(on_device, mesh.shape["wide"], mesh.shape["narrow"]),
        mesh=mesh,
        in_specs=(
            P("cfg", "wide", "narrow"),
            P(),
            P(None, "narrow"),
            P("narrow", "wide"),
            P("wide", "narrow"),
            P("narrow", None),
            P("wide", None),
            P(),
        ),
        out_specs=(P("cfg", "wide", "narrow"), P("wide", None)),
        check_vma=False,
    )
```

```python
import functools

import jax
import jax.numpy as jnp
import numpy as np
from jax import lax
from jax.experimental import pallas as pl
from jax.experimental.pallas import tpu as pltpu
from jax.sharding import PartitionSpec as P

TEXT = 226
EPS = 1e-05
GUIDANCE = 6.0
MESH = pl.DeviceIdType.MESH
F32 = jnp.float32
BF16 = jnp.bfloat16
I32 = jnp.int32


def alpha_table():
    start_root = 0.00085**0.5
    end_root = 0.012**0.5
    roots = start_root + (end_root - start_root) * np.arange(1000) / 999.0
    table = np.zeros((8, 128), np.float32)
    table.reshape(-1)[:1000] = np.cumprod(1.0 - roots * roots)
    return table


def dot(a, b):
    return jnp.dot(a, b, preferred_element_type=F32)


def dot_nt(a, b):
    return lax.dot_general(a, b, (((1,), (1,)), ((), ())), preferred_element_type=F32)


def iota(shape, dim):
    return lax.broadcasted_iota(I32, shape, dim)


def one_hot(condition):
    return jnp.where(condition, 1.0, 0.0).astype(BF16)


def body(
    sizes,
    split_ref,
    time_ref,
    hidden_ref,
    latent_ref,
    alpha_ref,
    mod_ref,
    w1_ref,
    w2_ref,
    ow_ref,
    out_ref,
    clean_ref,
    slab_s,
    slab_y,
    slab_r,
    xr,
    modg,
    owg,
    w1g,
    w2g,
    nst,
    gx,
    spread,
    xa,
    hid,
    act,
    sib_s,
    sib_r,
    ring_s,
    ring_r,
    tot,
    es,
    er,
    ffb,
    lo,
    back_s,
    back_z,
    back_r,
    vel_s,
    vel_r,
    a_s,
    a_r,
    az_s,
    az_r,
    b_s,
    b_r,
    bz_s,
    bz_r,
    y_s,
    y_r,
    w_s,
    w_r,
    loc,
    e_s,
    e_r,
    ag_s,
    ag_r,
    sb_s,
    sb_r,
    pr_s,
    pr_r,
    rg_s,
    rg_r,
    f_s,
    f_r,
    c_s,
    c_r,
):
    nz, ny, q, gr, bl, ff, cap, patch = sizes
    feats = ny * bl
    hb = bl // 2
    groups = ny * nz
    la, lb = nz // 2, nz - 1 - nz // 2
    cfg = lax.axis_index("cfg")
    w = lax.axis_index("wide")
    n = lax.axis_index("narrow")
    core = lax.rem(w, 2)
    z = lax.rem(w // 2, nz)
    xh = w // (2 * nz)
    d = 1 - 2 * core

    def wide_of(xh_, z_, core_):
        return xh_ * (2 * nz) + z_ * 2 + core_

    def zmod(v):
        return lax.rem(v + 2 * nz, nz)

    def yid(k):
        return lax.rem(n + k, ny)

    sib = (cfg, wide_of(xh, z, 1 - core), n)
    xpart = (cfg, wide_of(1 - xh, z, core), n)
    diag = (cfg, wide_of(1 - xh, z, 1 - core), n)
    znext = (cfg, wide_of(xh, zmod(z + d), core), n)
    zprev = (cfg, wide_of(xh, zmod(z - d), core), n)
    cpart = (1 - cfg, w, n)

    def ypeer(k):
        return (cfg, w, yid(k))

    def zpeer(k):
        return (cfg, wide_of(xh, zmod(z + k), core), n)

    def rcopy(src, dst, ssem, rsem, dev):
        return pltpu.make_async_remote_copy(
            src_ref=src, dst_ref=dst, send_sem=ssem, recv_sem=rsem, device_id=dev, device_id_type=MESH
        )

    def arrived(dst, rsem):
        rcopy(dst, dst, rsem, rsem, sib).wait_recv()

    def sent(src, ssem):
        rcopy(src, src, ssem, ssem, sib).wait_send()

    def signal(dev):
        pl.semaphore_signal(barrier, inc=1, device_id=dev, device_id_type=MESH)

    def times(count, action, first=0):
        def step(k, carry):
            action(k)
            return carry

        lax.fori_loop(first, count, step, 0)

    barrier = pltpu.get_barrier_semaphore()
    for dev in (ypeer(1), ypeer(2), ypeer(3), sib, xpart, diag, cpart):
        signal(dev)
    times(nz, lambda k: signal(zpeer(k)), 1)

    own = [(mod_ref, modg.at[n]), (w1_ref, w1g.at[n]), (w2_ref, w2g.at[n]), (ow_ref, owg.at[n])]
    for i, (src, dst) in enumerate(own):
        pltpu.make_async_copy(src, dst, loc.at[i]).start()

    def rows_of(i, size):
        return pl.ds(pl.multiple_of(i * size, size), size)

    offset = jnp.int32(0)
    count = jnp.int32(0)
    for b in range(split_ref.shape[0]):
        value = split_ref[b]
        offset = offset + jnp.where(b < w, value, 0)
        count = count + jnp.where(b == w, value, 0)
    row = iota((groups * 8, cap), 0)
    residue = (row >> 3) * 4 + (row & 3)
    hit = residue == ((iota((groups * 8, cap), 1) + offset) & (cap - 1))
    low = (row & 4) == 0
    slabs = dot(one_hot(hit & low), hidden_ref[:, :hb]) + dot(one_hot(hit & ~low), hidden_ref[:, hb:])
    slab_s[...] = slabs.reshape(ny, nz, 8, hb).astype(BF16)
    pl.semaphore_wait(barrier, 7 + nz - 1)

    for k in (1, 3, 2):
        rcopy(slab_s.at[yid(k)], slab_y.at[n], a_s.at[k - 1], a_r.at[k - 1], ypeer(k)).start()
    for k in (1, 3, 2):
        rcopy(mod_ref, modg.at[n], y_s.at[0, k - 1], y_r.at[0, k - 1], ypeer(k)).start()
    slab_y[n] = slab_s[n]
    weights = [(w1_ref, w1g, bl // 2), (w2_ref, w2g, ff // 2)]

    def weight_out(i):
        src, dst, _ = weights[i]
        rcopy(src, dst.at[n], w_s.at[i, 0], w_r.at[i, 0], ypeer(1)).start()
        rcopy(src, dst.at[n], w_s.at[i, 1], w_r.at[i, 1], ypeer(3)).start()

    def weight_on(i):
        _, dst, part = weights[i]
        pltpu.make_async_copy(own[1 + i][0], own[1 + i][1], loc.at[1 + i]).wait()
        arrived(dst.at[yid(3)], w_r.at[i, 0])
        first = dst.at[yid(3), pl.ds(0, part), :]
        rcopy(first, first, w_s.at[i, 2], w_r.at[i, 2], ypeer(1)).start()
        arrived(dst.at[yid(1)], w_r.at[i, 1])
        second = dst.at[yid(1), pl.ds(part, part), :]
        rcopy(second, second, w_s.at[i, 3], w_r.at[i, 3], ypeer(3)).start()

    def weight_in(i):
        _, dst, part = weights[i]
        arrived(dst.at[yid(2), pl.ds(0, part), :], w_r.at[i, 2])
        arrived(dst.at[yid(2), pl.ds(part, part), :], w_r.at[i, 3])

    weight_out(0)
    for k in (1, 2, 3):
        arrived(slab_y.at[yid(ny - k)], a_r.at[k - 1])

    def slab_on(k):
        zt = zmod(z + k)
        rcopy(slab_y.at[:, zt], slab_r.at[:, z], az_s.at[k - 1], az_r.at[k - 1], zpeer(k)).start()

    times(nz, slab_on, 1)
    weight_out(1)
    for k in (1, 3, 2):
        rcopy(ow_ref, owg.at[n], y_s.at[1, k - 1], y_r.at[1, k - 1], ypeer(k)).start()
    for b in range(ny):
        slab_r[b, z] = slab_y[b, z]
    hid[...] = jnp.zeros_like(hid)

    def slot_table(shape, dim):
        index = iota(shape, dim)
        member = index // q
        inner = index - member * q
        block = (member >> 1) * (2 * nz) + (inner >> 2) * 2 + (member & 1)
        off = jnp.zeros(shape, I32)
        cnt = jnp.zeros(shape, I32)
        for b in range(split_ref.shape[0]):
            value = split_ref[b]
            off = off + jnp.where(block > b, value, 0)
            cnt = cnt + jnp.where(block == b, value, 0)
        lane = inner & 3
        inside = ((n * nz + z) * 4 + lane - off) & (cap - 1)
        position = off + inside
        live = inside < cnt
        spot = jnp.where(live, lane * (gr // 4) + position // cap, -1)
        return live, position, spot

    lane_spot = slot_table((1, 4 * q), 1)[2]
    compact = one_hot(iota((gr, 4 * q), 0) == lane_spot)
    row_live, row_position, row_spot = slot_table((4 * q, 1), 0)
    spread[...] = jnp.where(iota((4 * q, gr), 1) == row_spot, 1.0, 0.0)
    member = xh * 2 + core
    state = jnp.where(row_live, jnp.where(row_position < TEXT, 2, 1), 0)
    tables = jnp.zeros((q, 1), I32)
    for i in range(4):
        tables = tables + jnp.where(member == i, state[i * q : (i + 1) * q], 0)
    live = tables > 0
    text = tables == 2

    def pick(b, row_text, row_video):
        return jnp.where(text, modg[b, pl.ds(row_text, 1), :], modg[b, pl.ds(row_video, 1), :])

    def stats(total, squares):
        average = total / feats
        variance = squares / feats - average * average
        return average, lax.rsqrt(variance + EPS)

    unrow = iota((q, 2 * q), 0)
    uncol = iota((q, 2 * q), 1)
    unhit = ((unrow >> 2) == (uncol >> 3)) & ((unrow & 3) == (uncol & 3))
    unlow = (uncol & 4) == 0
    take_low = one_hot(unhit & unlow)
    take_high = one_hot(unhit & ~unlow)
    times(nz, lambda k: arrived(slab_r.at[:, zmod(z - k)], az_r.at[k - 1]), 1)
    total = jnp.zeros((q, 1), F32)
    squares = jnp.zeros((q, 1), F32)
    for b in range(ny):
        v = slab_r[b].astype(F32).reshape(nz * 8, hb).astype(BF16)
        for part, take in ((0, take_low), (1, take_high)):
            u = dot(take, v)
            xr[b, :, part * hb : (part + 1) * hb] = u.astype(BF16)
            total = total + jnp.sum(u, -1, keepdims=True)
            squares = squares + jnp.sum(u * u, -1, keepdims=True)
    average, scale = stats(total, squares)
    pltpu.make_async_copy(own[0][0], own[0][1], loc.at[0]).wait()
    for k in (1, 2, 3):
        arrived(modg.at[yid(ny - k)], y_r.at[0, k - 1])
    for b in range(ny):
        v = xr[b].astype(F32)
        nst[b] = ((v - average) * scale * (1.0 + pick(b, 4, 1)) + pick(b, 3, 0)).astype(BF16)

    mine = 2 * core
    other = 2 * (1 - core)
    own_rows = rows_of(member, q)
    mates = [(sib, xh * 2 + 1 - core, other), (xpart, (1 - xh) * 2 + core, mine), (diag, (1 - xh) * 2 + 1 - core, other)]
    for i in (1, 2, 0):
        dev, _, blk = mates[i]
        rcopy(nst.at[pl.ds(blk, 2)], gx.at[:, own_rows, :], e_s.at[i], e_r.at[i], dev).start()
    for j in range(2):
        gx[j, own_rows, :] = nst[mine + j]
    weight_on(0)
    for i in range(3):
        arrived(gx.at[:, rows_of(mates[i][1], q), :], e_r.at[i])
    for j in range(2):
        xa[z, mine + j] = dot(compact, gx[j]).astype(BF16)

    def side(o, first):
        return xa.at[o, pl.ds(first, 2)]

    def relay(o, j, sem, dev):
        rcopy(xa.at[o, mine + j], xa.at[o, mine + j], ag_s.at[sem, j], ag_r.at[sem, j], dev).start()

    def share(u):
        o = zmod(z + d * u)
        rcopy(side(o, mine), side(o, mine), sb_s.at[u % nz], sb_r.at[u % nz], sib).start()

    def work(u):
        o = zmod(z + d * u)
        hid[o] = hid[o] + (dot(xa[o, mine], w1g[mine]) + dot(xa[o, mine + 1], w1g[mine + 1]))
        p = zmod(z - d * u)
        arrived(side(p, other), sb_r.at[zmod(u)])
        hid[p] = hid[p] + (dot(xa[p, other], w1g[other]) + dot(xa[p, other + 1], w1g[other + 1]))

    def gelu(o):
        v = hid[o]
        act[o] = (0.5 * v * (1.0 + jnp.tanh(0.7978845608 * (v + 0.044715 * (v * v * v))))).astype(BF16)

    for s in range(la):
        for j in range(2):
            if s > 0:
                arrived(xa.at[zmod(z - d * s), mine + j], ag_r.at[s - 1, j])
            relay(zmod(z - d * s), j, s, znext)
            if 0 < s <= lb:
                arrived(xa.at[zmod(z + d * s), mine + j], ag_r.at[la + s - 1, j])
            if s < lb:
                relay(zmod(z + d * s), j, la + s, zprev)
        share(-s)
        if 0 < s <= lb:
            share(s)
        if s == la - 1:
            weight_on(1)
            weight_in(0)
            work(0)

            def pair(k):
                work(k)
                work(-k)

            times(la, pair, 1)
    for j in range(2):
        arrived(xa.at[zmod(z - d * la), mine + j], ag_r.at[la - 1, j])
    share(-la)
    for s in range(la, lb + 1):
        for j in range(2):
            arrived(xa.at[zmod(z + d * s), mine + j], ag_r.at[la + s - 1, j])
        share(s)
    for u in range(la, nz - la + 1):
        work(u)
    times(nz, gelu)

    far = lax.rem(n + 2, ny)

    def blk_of(side_, b):
        near = side_ == n // 2
        first = jnp.where(near, n, far + 1 - 2 * lax.rem(far, 2))
        second = jnp.where(near, n + 1 - 2 * lax.rem(n, 2), far)
        return first if b == 0 else second

    order = []
    for s in range(la):
        order.append(("next", s, la - s))
        if s < lb:
            order.append(("prev", s, -(lb - s)))
    order.append(("stay", 0, 0))
    slot_of = {(kind, s): t for t, (kind, s, _) in enumerate(order)}

    def sib_part(t, b):
        p = zmod(z - d * order[t][2])
        sib_s[t, b] = dot(act[p], w2g[blk_of(1 - core, b)]).astype(BF16)
        rcopy(sib_s.at[t, b], sib_r.at[t, b], pr_s.at[t, b], pr_r.at[t, b], sib).start()

    def ring_part(t, b):
        kind, s, u = order[t]
        part = dot(act[zmod(z + d * u)], w2g[blk_of(core, b)])
        arrived(sib_r.at[t, b], pr_r.at[t, b])
        part = part + sib_r[t, b].astype(F32)
        if kind == "stay":
            before = [slot_of[("next", la - 1)]] + ([slot_of[("prev", lb - 1)]] if lb else [])
        else:
            before = [slot_of[(kind, s - 1)]] if s else []
        for p in before:
            arrived(ring_r.at[p, b], rg_r.at[p, b])
            part = part + ring_r[p, b].astype(F32)
        if kind == "stay":
            tot[b] = part.astype(BF16)
            for i in range(3):
                dev, index, _ = mates[i]
                es[i, b] = dot(spread[rows_of(index, q), :].astype(BF16), tot[b]).astype(BF16)
                rcopy(es.at[i, b], er.at[i, b], f_s.at[i, b], f_r.at[i, b], dev).start()
            return
        ring_s[t, b] = part.astype(BF16)
        rcopy(
            ring_s.at[t, b], ring_r.at[t, b], rg_s.at[t, b], rg_r.at[t, b], znext if kind == "next" else zprev
        ).start()

    stages = {}
    for t, (kind, s, _) in enumerate(order):
        stages.setdefault(la if kind == "stay" else s, []).append(t)
    lag = 2
    events = []
    for step in range(la + 1 + lag):
        for b in range(2):
            at = step - lag * b
            if 0 <= at <= la:
                events += [(t, b) for t in stages[at]]
    ahead = 2
    for t, b in events[:ahead]:
        sib_part(t, b)
    needs_far = False
    for i, (t, b) in enumerate(events):
        if i + ahead < len(events):
            if events[i + ahead][1] == 1 and not needs_far:
                weight_in(1)
                needs_far = True
            sib_part(*events[i + ahead])
        ring_part(t, b)

    for b in range(2):
        arrived(er.at[1, b], f_r.at[1, b])
        ffb[blk_of(core, b)] = dot(spread[own_rows, :].astype(BF16), tot[b]) + er[1, b].astype(F32)
    for b in range(2):
        arrived(er.at[0, b], f_r.at[0, b])
        arrived(er.at[2, b], f_r.at[2, b])
        ffb[blk_of(1 - core, b)] = er[0, b].astype(F32) + er[2, b].astype(F32)
    total = jnp.zeros((q, 1), F32)
    squares = jnp.zeros((q, 1), F32)
    for b in range(ny):
        v = xr[b].astype(F32) + pick(b, 5, 2) * ffb[b]
        v = jnp.where(live, v, 0.0).astype(BF16)
        lo[b] = v
        v = v.astype(F32)
        total = total + jnp.sum(v, -1, keepdims=True)
        squares = squares + jnp.sum(v * v, -1, keepdims=True)
    average, scale = stats(total, squares)
    pltpu.make_async_copy(own[3][0], own[3][1], loc.at[3]).wait()
    for k in (1, 2, 3):
        arrived(owg.at[yid(ny - k)], y_r.at[1, k - 1])
    velocity = jnp.zeros((q, patch), F32)
    for b in range(ny):
        v = (lo[b].astype(F32) - average) * scale
        v = (v * (1.0 + modg[b, pl.ds(7, 1), :]) + modg[b, pl.ds(6, 1), :]).astype(BF16)
        velocity = velocity + dot_nt(v, owg[b])
    velocity = velocity * jnp.where(cfg == 0, GUIDANCE, 1.0 - GUIDANCE)

    coarse = velocity.astype(BF16)
    fine = (velocity - coarse.astype(F32)).astype(BF16)
    backrow = iota((2 * q, q), 0)
    backcol = iota((2 * q, q), 1)
    backhit = ((backcol >> 2) == (backrow >> 3)) & ((backcol & 3) == (backrow & 3))
    backlow = (backrow & 4) == 0
    put_low = one_hot(backhit & backlow)
    put_high = one_hot(backhit & ~backlow)
    terms = dot(put_low, jnp.concatenate([coarse, fine], axis=1)).reshape(nz, 8, 2 * patch).astype(BF16)
    for b in range(ny):
        v = dot(put_low, lo[b, :, :hb]) + dot(put_high, lo[b, :, hb:])
        back_s[b, :, :, :hb] = v.reshape(nz, 8, hb).astype(BF16)
        back_s[b, :, :, hb:] = terms

    def back_out(k):
        zt = zmod(z + k)
        rcopy(back_s.at[:, zt], back_z.at[:, z], bz_s.at[k - 1], bz_r.at[k - 1], zpeer(k)).start()

    times(nz, back_out, 1)
    for b in range(ny):
        back_z[b, z] = back_s[b, z]

    column = iota((cap, groups * 8), 1)
    undo = ((column >> 3) * 4 + (column & 3)) == ((iota((cap, groups * 8), 0) + offset) & (cap - 1))
    undo_low = one_hot(undo & ((column & 4) == 0))
    undo_high = one_hot(undo & ((column & 4) != 0))
    index = iota((8, 128), 0) * 128 + iota((8, 128), 1)
    alpha = jnp.where(index == time_ref[0], alpha_ref[...], 0.0)
    alpha = jnp.sum(jnp.sum(alpha, 0, keepdims=True), 1, keepdims=True)
    scaled = jnp.sqrt(alpha) * latent_ref[...]
    factor = jnp.sqrt(1.0 - alpha)
    lanes = iota((1, cap), 1)
    video = (lanes < count) & (lanes + offset >= TEXT)
    times(nz, lambda k: arrived(back_z.at[:, zmod(z - k)], bz_r.at[k - 1]), 1)
    for k in (1, 3, 2):
        rcopy(back_z.at[yid(k)], back_r.at[n], b_s.at[k - 1], b_r.at[k - 1], ypeer(k)).start()
    back_r[n] = back_z[n]
    for k in (1, 2, 3):
        arrived(back_r.at[yid(ny - k)], b_r.at[k - 1])
    v = back_r[:, :, :, hb:].astype(F32).reshape(groups * 8, 2 * patch).astype(BF16)
    v = dot(undo_low, v).T
    vel_s[...] = v[:patch] + v[patch:]
    rcopy(vel_s, vel_r, c_s.at[0], c_r.at[0], cpart).start()
    v = back_r[:, :, :, :hb].astype(F32).reshape(groups * 8, hb).astype(BF16)
    out_ref[:, :hb] = dot(undo_low, v).astype(BF16)
    out_ref[:, hb:] = dot(undo_high, v).astype(BF16)

    def slabs_sent(k):
        zt = zmod(z + k)
        sent(slab_y.at[:, zt], az_s.at[k - 1])
        sent(back_s.at[:, zt], bz_s.at[k - 1])

    times(nz, slabs_sent, 1)
    for k in (1, 2, 3):
        sent(slab_s.at[yid(k)], a_s.at[k - 1])
        sent(back_z.at[yid(k)], b_s.at[k - 1])
        sent(mod_ref, y_s.at[0, k - 1])
        sent(ow_ref, y_s.at[1, k - 1])
    for i, (src, dst, part) in enumerate(weights):
        sent(src, w_s.at[i, 0])
        sent(src, w_s.at[i, 1])
        sent(dst.at[yid(3), pl.ds(0, part), :], w_s.at[i, 2])
        sent(dst.at[yid(1), pl.ds(part, part), :], w_s.at[i, 3])
    for i in range(3):
        sent(nst.at[pl.ds(mates[i][2], 2)], e_s.at[i])
        for b in range(2):
            sent(es.at[i, b], f_s.at[i, b])
    for s in range(la):
        for j in range(2):
            sent(xa.at[zmod(z - d * s), mine + j], ag_s.at[s, j])
    for s in range(lb):
        for j in range(2):
            sent(xa.at[zmod(z + d * s), mine + j], ag_s.at[la + s, j])
    for t in range(nz):
        sent(side(zmod(z + d * t), mine), sb_s.at[t])
        for b in range(2):
            sent(sib_s.at[t, b], pr_s.at[t, b])
            if t < nz - 1:
                sent(ring_s.at[t, b], rg_s.at[t, b])
    arrived(vel_r, c_r.at[0])
    clean_ref[...] = jnp.where(video, scaled - factor * (vel_s[...] + vel_r[...]), 0.0)
    sent(vel_s, c_s.at[0])


def on_device(n_wide, n_narrow, hidden, split_table, modulation, w1, w2, ow, latent, timestep):
    cap, bl = hidden.shape[1:]
    ff = w1.shape[1]
    patch = ow.shape[1]
    ny = n_narrow
    nz = n_wide // 4
    q = cap // ny
    gr = n_wide * 2
    sizes = (nz, ny, q, gr, bl, ff, cap, patch)
    hb = bl // 2
    dma = pltpu.SemaphoreType.DMA
    vm = pltpu.VMEM
    scratch = [
        vm((ny, nz, 8, hb), BF16),
        vm((ny, nz, 8, hb), BF16),
        vm((ny, nz, 8, hb), BF16),
        vm((ny, q, bl), BF16),
        vm((ny, 8, bl), F32),
        vm((ny, patch, bl), BF16),
        vm((ny, bl, ff), BF16),
        vm((ny, ff, bl), BF16),
        vm((ny, q, bl), BF16),
        vm((2, 4 * q, bl), BF16),
        vm((4 * q, gr), F32),
        vm((nz, ny, gr, bl), BF16),
        vm((nz, gr, ff), F32),
        vm((nz, gr, ff), BF16),
        vm((nz, 2, gr, bl), BF16),
        vm((nz, 2, gr, bl), BF16),
        vm((nz - 1, 2, gr, bl), BF16),
        vm((nz - 1, 2, gr, bl), BF16),
        vm((2, gr, bl), BF16),
        vm((3, 2, q, bl), BF16),
        vm((3, 2, q, bl), BF16),
        vm((ny, q, bl), F32),
        vm((ny, q, bl), BF16),
        vm((ny, nz, 8, hb + 2 * patch), BF16),
        vm((ny, nz, 8, hb + 2 * patch), BF16),
        vm((ny, nz, 8, hb + 2 * patch), BF16),
        vm((patch, cap), F32),
        vm((patch, cap), F32),
        dma((ny - 1,)),
        dma((ny - 1,)),
        dma((nz - 1,)),
        dma((nz - 1,)),
        dma((ny - 1,)),
        dma((ny - 1,)),
        dma((nz - 1,)),
        dma((nz - 1,)),
        dma((2, 3)),
        dma((2, 3)),
        dma((2, 4)),
        dma((2, 4)),
        dma((4,)),
        dma((3,)),
        dma((3,)),
        dma((nz - 1, 2)),
        dma((nz - 1, 2)),
        dma((nz,)),
        dma((nz,)),
        dma((nz, 2)),
        dma((nz, 2)),
        dma((nz - 1, 2)),
        dma((nz - 1, 2)),
        dma((3, 2)),
        dma((3, 2)),
        dma((1,)),
        dma((1,)),
    ]
    hbm = pl.BlockSpec(memory_space=pltpu.HBM)
    smem = pl.BlockSpec(memory_space=pltpu.SMEM)
    vmem = pl.BlockSpec(memory_space=pltpu.VMEM)
    layer_out, clean = pl.pallas_call(
        functools.partial(body, sizes),
        out_shape=(
            jax.ShapeDtypeStruct((cap, bl), BF16),
            jax.ShapeDtypeStruct((patch, cap), F32),
        ),
        in_specs=[smem, smem, vmem, vmem, vmem, hbm, hbm, hbm, hbm],
        out_specs=(vmem, vmem),
        scratch_shapes=scratch,
        compiler_params=pltpu.CompilerParams(
            collective_id=0, has_side_effects=True, vmem_limit_bytes=60 * 1024 * 1024
        ),
    )(
        split_table,
        timestep,
        hidden[0],
        latent.T,
        jnp.asarray(alpha_table()),
        modulation,
        w1,
        w2,
        ow.T,
    )
    return (layer_out[None], clean.T)


def solution(mesh):
    return jax.shard_map(
        functools.partial(on_device, mesh.shape["wide"], mesh.shape["narrow"]),
        mesh=mesh,
        in_specs=(
            P("cfg", "wide", "narrow"),
            P(),
            P(None, "narrow"),
            P("narrow", "wide"),
            P("wide", "narrow"),
            P("narrow", None),
            P("wide", None),
            P(),
        ),
        out_specs=(P("cfg", "wide", "narrow"), P("wide", None)),
        check_vma=False,
    )
```

```python
import functools

import jax
import jax.numpy as jnp
import numpy as np
from jax import lax
from jax.experimental import pallas as pl
from jax.experimental.pallas import tpu as pltpu
from jax.sharding import PartitionSpec as P

TEXT = 226
EPS = 1e-05
GUIDANCE = 6.0
MESH = pl.DeviceIdType.MESH
F32 = jnp.float32
BF16 = jnp.bfloat16
I32 = jnp.int32


def alpha_table():
    start_root = 0.00085**0.5
    end_root = 0.012**0.5
    roots = start_root + (end_root - start_root) * np.arange(1000) / 999.0
    table = np.zeros((8, 128), np.float32)
    table.reshape(-1)[:1000] = np.cumprod(1.0 - roots * roots)
    return table


def dot(a, b):
    return jnp.dot(a, b, preferred_element_type=F32)


def dot_nt(a, b):
    return lax.dot_general(a, b, (((1,), (1,)), ((), ())), preferred_element_type=F32)


def iota(shape, dim):
    return lax.broadcasted_iota(I32, shape, dim)


def one_hot(condition):
    return jnp.where(condition, 1.0, 0.0).astype(BF16)


def body(
    sizes,
    split_ref,
    time_ref,
    hidden_ref,
    latent_ref,
    alpha_ref,
    mod_ref,
    w1_ref,
    w2_ref,
    ow_ref,
    out_ref,
    clean_ref,
    slab_s,
    slab_r,
    xr,
    modg,
    owg,
    w1g,
    w2g,
    nst,
    gx,
    spread,
    xa,
    hid,
    act,
    sib_s,
    sib_r,
    ring_s,
    ring_r,
    tot,
    es,
    er,
    ffb,
    lo,
    back_s,
    back_r,
    vel_s,
    vel_r,
    a_s,
    a_r,
    b_s,
    b_r,
    y_s,
    y_r,
    w_s,
    w_r,
    loc,
    e_s,
    e_r,
    ag_s,
    ag_r,
    sb_s,
    sb_r,
    pr_s,
    pr_r,
    rg_s,
    rg_r,
    f_s,
    f_r,
    c_s,
    c_r,
):
    nz, ny, q, gr, bl, ff, cap, patch = sizes
    feats = ny * bl
    hb = bl // 2
    groups = ny * nz
    la, lb = nz // 2, nz - 1 - nz // 2
    cfg = lax.axis_index("cfg")
    w = lax.axis_index("wide")
    n = lax.axis_index("narrow")
    core = lax.rem(w, 2)
    z = lax.rem(w // 2, nz)
    xh = w // (2 * nz)
    d = 1 - 2 * core

    def wide_of(xh_, z_, core_):
        return xh_ * (2 * nz) + z_ * 2 + core_

    def zmod(v):
        return lax.rem(v + 2 * nz, nz)

    def yid(k):
        return lax.rem(n + k, ny)

    sib = (cfg, wide_of(xh, z, 1 - core), n)
    xpart = (cfg, wide_of(1 - xh, z, core), n)
    diag = (cfg, wide_of(1 - xh, z, 1 - core), n)
    znext = (cfg, wide_of(xh, zmod(z + d), core), n)
    zprev = (cfg, wide_of(xh, zmod(z - d), core), n)
    cpart = (1 - cfg, w, n)

    def ypeer(k):
        return (cfg, w, yid(k))

    def peer(k):
        m = lax.rem(n + k // nz, ny)
        zd = lax.rem(z + lax.rem(k, nz), nz)
        return m * nz + zd, (cfg, wide_of(xh, zd, core), m)

    def source(k):
        m = lax.rem(n + ny - k // nz, ny)
        zd = lax.rem(z + nz - lax.rem(k, nz), nz)
        return m * nz + zd

    def rcopy(src, dst, ssem, rsem, dev):
        return pltpu.make_async_remote_copy(
            src_ref=src, dst_ref=dst, send_sem=ssem, recv_sem=rsem, device_id=dev, device_id_type=MESH
        )

    def arrived(dst, rsem):
        rcopy(dst, dst, rsem, rsem, sib).wait_recv()

    def sent(src, ssem):
        rcopy(src, src, ssem, ssem, sib).wait_send()

    def signal(dev):
        pl.semaphore_signal(barrier, inc=1, device_id=dev, device_id_type=MESH)

    def times(count, action, first=0):
        def step(k, carry):
            action(k)
            return carry

        lax.fori_loop(first, count, step, 0)

    barrier = pltpu.get_barrier_semaphore()
    times(groups, lambda k: signal(peer(k)[1]), 1)
    for dev in (sib, xpart, diag, cpart):
        signal(dev)

    own = [(mod_ref, modg.at[n]), (w1_ref, w1g.at[n]), (w2_ref, w2g.at[n]), (ow_ref, owg.at[n])]
    for i, (src, dst) in enumerate(own):
        pltpu.make_async_copy(src, dst, loc.at[i]).start()

    def rows_of(i, size):
        return pl.ds(pl.multiple_of(i * size, size), size)

    offset = jnp.int32(0)
    count = jnp.int32(0)
    for b in range(split_ref.shape[0]):
        value = split_ref[b]
        offset = offset + jnp.where(b < w, value, 0)
        count = count + jnp.where(b == w, value, 0)
    row = iota((groups * 8, cap), 0)
    residue = (row >> 3) * 4 + (row & 3)
    hit = residue == ((iota((groups * 8, cap), 1) + offset) & (cap - 1))
    low = (row & 4) == 0
    slabs = dot(one_hot(hit & low), hidden_ref[:, :hb]) + dot(one_hot(hit & ~low), hidden_ref[:, hb:])
    slab_s[...] = slabs.reshape(groups, 8, hb).astype(BF16)
    pl.semaphore_wait(barrier, groups - 1 + 4)

    def slab_out(k):
        target, dev = peer(k)
        rcopy(slab_s.at[target], slab_r.at[n * nz + z], a_s.at[k - 1], a_r.at[k - 1], dev).start()

    times(groups, slab_out, 1)
    for k in (1, 3, 2):
        rcopy(mod_ref, modg.at[n], y_s.at[0, k - 1], y_r.at[0, k - 1], ypeer(k)).start()
    slab_r[n * nz + z] = slab_s[n * nz + z]
    weights = [(w1_ref, w1g, bl // 4), (w2_ref, w2g, ff // 4)]
    give, far_own = 3 * cfg, 2 * cfg

    def rows_at(i, first, quarters):
        part = weights[i][2]
        return pl.ds(pl.multiple_of(first * part, part), quarters * part)

    def piece(i, blk, first, quarters):
        return weights[i][1].at[blk, rows_at(i, first, quarters), :]

    sides = ((yid(3), ypeer(1)), (yid(1), ypeer(3)))

    def pass_on(i, blk, first, quarters, sem, dev):
        rcopy(piece(i, blk, first, quarters), piece(i, blk, first, quarters), w_s.at[i, sem], w_r.at[i, sem], dev).start()

    def weight_out(i):
        src = weights[i][0]
        for sem, first, quarters in ((0, give, 1), (2, 1, 2)):
            for k in range(2):
                rcopy(
                    src.at[rows_at(i, first, quarters), :],
                    piece(i, n, first, quarters),
                    w_s.at[i, sem + k],
                    w_r.at[i, sem + k],
                    sides[k][1],
                ).start()

    def weight_give(i):
        for k in range(2):
            arrived(piece(i, sides[k][0], give, 1), w_r.at[i, k])
            pass_on(i, sides[k][0], give, 1, 4 + k, cpart)

    def weight_on(i):
        for k in range(2):
            arrived(piece(i, sides[k][0], 1, 2), w_r.at[i, 2 + k])
            pass_on(i, sides[k][0], far_own + k, 1, 6 + k, sides[k][1])

    def weight_far(i):
        for k in range(2):
            arrived(piece(i, yid(2), far_own + k, 1), w_r.at[i, 6 + k])
        pass_on(i, yid(2), far_own, 2, 8, cpart)

    def weight_near_in(i):
        pltpu.make_async_copy(own[1 + i][0], own[1 + i][1], loc.at[1 + i]).wait()
        for k in range(2):
            arrived(piece(i, sides[k][0], 3 - give, 1), w_r.at[i, 4 + k])

    def weight_far_in(i):
        arrived(piece(i, yid(2), 2 - far_own, 2), w_r.at[i, 8])

    def weights_sent(i):
        for k in range(2):
            sent(weights[i][0].at[rows_at(i, give, 1), :], w_s.at[i, k])
            sent(weights[i][0].at[rows_at(i, 1, 2), :], w_s.at[i, 2 + k])
            sent(piece(i, sides[k][0], give, 1), w_s.at[i, 4 + k])
            sent(piece(i, sides[k][0], far_own + k, 1), w_s.at[i, 6 + k])
        sent(piece(i, yid(2), far_own, 2), w_s.at[i, 8])

    weight_out(0)
    for k in (1, 3, 2):
        rcopy(ow_ref, owg.at[n], y_s.at[1, k - 1], y_r.at[1, k - 1], ypeer(k)).start()
    hid[...] = jnp.zeros_like(hid)

    def slot_table(shape, dim):
        index = iota(shape, dim)
        member = index // q
        inner = index - member * q
        block = (member >> 1) * (2 * nz) + (inner >> 2) * 2 + (member & 1)
        off = jnp.zeros(shape, I32)
        cnt = jnp.zeros(shape, I32)
        for b in range(split_ref.shape[0]):
            value = split_ref[b]
            off = off + jnp.where(block > b, value, 0)
            cnt = cnt + jnp.where(block == b, value, 0)
        lane = inner & 3
        inside = ((n * nz + z) * 4 + lane - off) & (cap - 1)
        position = off + inside
        live = inside < cnt
        spot = jnp.where(live, lane * (gr // 4) + position // cap, -1)
        return live, position, spot

    lane_spot = slot_table((1, 4 * q), 1)[2]
    compact = one_hot(iota((gr, 4 * q), 0) == lane_spot)
    row_live, row_position, row_spot = slot_table((4 * q, 1), 0)
    spread[...] = jnp.where(iota((4 * q, gr), 1) == row_spot, 1.0, 0.0)
    member = xh * 2 + core
    state = jnp.where(row_live, jnp.where(row_position < TEXT, 2, 1), 0)
    tables = jnp.zeros((q, 1), I32)
    for i in range(4):
        tables = tables + jnp.where(member == i, state[i * q : (i + 1) * q], 0)
    live = tables > 0
    text = tables == 2

    def pick(b, row_text, row_video):
        return jnp.where(text, modg[b, pl.ds(row_text, 1), :], modg[b, pl.ds(row_video, 1), :])

    def stats(total, squares):
        average = total / feats
        variance = squares / feats - average * average
        return average, lax.rsqrt(variance + EPS)

    unrow = iota((q, 2 * q), 0)
    uncol = iota((q, 2 * q), 1)
    unhit = ((unrow >> 2) == (uncol >> 3)) & ((unrow & 3) == (uncol & 3))
    unlow = (uncol & 4) == 0
    take_low = one_hot(unhit & unlow)
    take_high = one_hot(unhit & ~unlow)
    weight_give(0)
    times(groups, lambda k: arrived(slab_r.at[source(k)], a_r.at[k - 1]), 1)
    total = jnp.zeros((q, 1), F32)
    squares = jnp.zeros((q, 1), F32)
    for b in range(ny):
        v = slab_r[b * nz : (b + 1) * nz].astype(F32).reshape(nz * 8, hb).astype(BF16)
        for part, take in ((0, take_low), (1, take_high)):
            u = dot(take, v)
            xr[b, :, part * hb : (part + 1) * hb] = u.astype(BF16)
            total = total + jnp.sum(u, -1, keepdims=True)
            squares = squares + jnp.sum(u * u, -1, keepdims=True)
    average, scale = stats(total, squares)
    pltpu.make_async_copy(own[0][0], own[0][1], loc.at[0]).wait()
    for k in (1, 2, 3):
        arrived(modg.at[yid(ny - k)], y_r.at[0, k - 1])
    for b in range(ny):
        v = xr[b].astype(F32)
        nst[b] = ((v - average) * scale * (1.0 + pick(b, 4, 1)) + pick(b, 3, 0)).astype(BF16)

    mine = 2 * core
    other = 2 * (1 - core)
    own_rows = rows_of(member, q)
    mates = [(sib, xh * 2 + 1 - core, other), (xpart, (1 - xh) * 2 + core, mine), (diag, (1 - xh) * 2 + 1 - core, other)]
    for i in (1, 2, 0):
        dev, _, blk = mates[i]
        rcopy(nst.at[pl.ds(blk, 2)], gx.at[:, own_rows, :], e_s.at[i], e_r.at[i], dev).start()
    for j in range(2):
        gx[j, own_rows, :] = nst[mine + j]
    weight_on(0)
    weight_out(1)
    for i in range(3):
        arrived(gx.at[:, rows_of(mates[i][1], q), :], e_r.at[i])
    for j in range(2):
        xa[z, mine + j] = dot(compact, gx[j]).astype(BF16)

    def side(o, first):
        return xa.at[o, pl.ds(first, 2)]

    def relay(o, j, sem, dev):
        rcopy(xa.at[o, mine + j], xa.at[o, mine + j], ag_s.at[sem, j], ag_r.at[sem, j], dev).start()

    def share(u):
        o = zmod(z + d * u)
        rcopy(side(o, mine), side(o, mine), sb_s.at[u % nz], sb_r.at[u % nz], sib).start()

    def work(u):
        o = zmod(z + d * u)
        hid[o] = hid[o] + (dot(xa[o, mine], w1g[mine]) + dot(xa[o, mine + 1], w1g[mine + 1]))
        p = zmod(z - d * u)
        arrived(side(p, other), sb_r.at[zmod(u)])
        hid[p] = hid[p] + (dot(xa[p, other], w1g[other]) + dot(xa[p, other + 1], w1g[other + 1]))

    def gelu(o):
        v = hid[o]
        act[o] = (0.5 * v * (1.0 + jnp.tanh(0.7978845608 * (v + 0.044715 * (v * v * v))))).astype(BF16)

    plan = ((0, weight_far, 0), (1, weight_give, 1), (2, weight_on, 1), (3, weight_far, 1))
    for s in range(la):
        for j in range(2):
            if s > 0:
                arrived(xa.at[zmod(z - d * s), mine + j], ag_r.at[s - 1, j])
            relay(zmod(z - d * s), j, s, znext)
            if 0 < s <= lb:
                arrived(xa.at[zmod(z + d * s), mine + j], ag_r.at[la + s - 1, j])
            if s < lb:
                relay(zmod(z + d * s), j, la + s, zprev)
        share(-s)
        if 0 < s <= lb:
            share(s)
        for at, action, i in plan:
            if s == min(at, la - 1):
                action(i)
        if s == la - 1:
            weight_near_in(0)
            weight_far_in(0)
            work(0)

            def pair(k):
                work(k)
                work(-k)

            times(la, pair, 1)
    for j in range(2):
        arrived(xa.at[zmod(z - d * la), mine + j], ag_r.at[la - 1, j])
    share(-la)
    for s in range(la, lb + 1):
        for j in range(2):
            arrived(xa.at[zmod(z + d * s), mine + j], ag_r.at[la + s - 1, j])
        share(s)
    for u in range(la, nz - la + 1):
        work(u)
    times(nz, gelu)

    far = lax.rem(n + 2, ny)

    def blk_of(side_, b):
        near = side_ == n // 2
        first = jnp.where(near, n, far + 1 - 2 * lax.rem(far, 2))
        second = jnp.where(near, n + 1 - 2 * lax.rem(n, 2), far)
        return first if b == 0 else second

    order = []
    for s in range(la):
        order.append(("next", s, la - s))
        if s < lb:
            order.append(("prev", s, -(lb - s)))
    order.append(("stay", 0, 0))
    slot_of = {(kind, s): t for t, (kind, s, _) in enumerate(order)}

    def sib_part(t, b):
        p = zmod(z - d * order[t][2])
        sib_s[t, b] = dot(act[p], w2g[blk_of(1 - core, b)]).astype(BF16)
        rcopy(sib_s.at[t, b], sib_r.at[t, b], pr_s.at[t, b], pr_r.at[t, b], sib).start()

    def ring_part(t, b):
        kind, s, u = order[t]
        part = dot(act[zmod(z + d * u)], w2g[blk_of(core, b)])
        arrived(sib_r.at[t, b], pr_r.at[t, b])
        part = part + sib_r[t, b].astype(F32)
        if kind == "stay":
            before = [slot_of[("next", la - 1)]] + ([slot_of[("prev", lb - 1)]] if lb else [])
        else:
            before = [slot_of[(kind, s - 1)]] if s else []
        for p in before:
            arrived(ring_r.at[p, b], rg_r.at[p, b])
            part = part + ring_r[p, b].astype(F32)
        if kind == "stay":
            tot[b] = part.astype(BF16)
            for i in range(3):
                dev, index, _ = mates[i]
                es[i, b] = dot(spread[rows_of(index, q), :].astype(BF16), tot[b]).astype(BF16)
                rcopy(es.at[i, b], er.at[i, b], f_s.at[i, b], f_r.at[i, b], dev).start()
            return
        ring_s[t, b] = part.astype(BF16)
        rcopy(
            ring_s.at[t, b], ring_r.at[t, b], rg_s.at[t, b], rg_r.at[t, b], znext if kind == "next" else zprev
        ).start()

    stages = {}
    for t, (kind, s, _) in enumerate(order):
        stages.setdefault(la if kind == "stay" else s, []).append(t)
    lag = 0
    events = []
    for step in range(la + 1 + lag):
        for b in range(2):
            at = step - lag * b
            if 0 <= at <= la:
                events += [(t, b) for t in stages[at]]
    ahead = 2
    weight_near_in(1)
    for t, b in events[:ahead]:
        sib_part(t, b)
    needs_far = False
    for i, (t, b) in enumerate(events):
        if i + ahead < len(events):
            if events[i + ahead][1] == 1 and not needs_far:
                weight_far_in(1)
                needs_far = True
            sib_part(*events[i + ahead])
        ring_part(t, b)

    for b in range(2):
        arrived(er.at[1, b], f_r.at[1, b])
        ffb[blk_of(core, b)] = dot(spread[own_rows, :].astype(BF16), tot[b]) + er[1, b].astype(F32)
    for b in range(2):
        arrived(er.at[0, b], f_r.at[0, b])
        arrived(er.at[2, b], f_r.at[2, b])
        ffb[blk_of(1 - core, b)] = er[0, b].astype(F32) + er[2, b].astype(F32)
    total = jnp.zeros((q, 1), F32)
    squares = jnp.zeros((q, 1), F32)
    for b in range(ny):
        v = xr[b].astype(F32) + pick(b, 5, 2) * ffb[b]
        v = jnp.where(live, v, 0.0).astype(BF16)
        lo[b] = v
        v = v.astype(F32)
        total = total + jnp.sum(v, -1, keepdims=True)
        squares = squares + jnp.sum(v * v, -1, keepdims=True)
    average, scale = stats(total, squares)
    pltpu.make_async_copy(own[3][0], own[3][1], loc.at[3]).wait()
    for k in (1, 2, 3):
        arrived(owg.at[yid(ny - k)], y_r.at[1, k - 1])
    velocity = jnp.zeros((q, patch), F32)
    for b in range(ny):
        v = (lo[b].astype(F32) - average) * scale
        v = (v * (1.0 + modg[b, pl.ds(7, 1), :]) + modg[b, pl.ds(6, 1), :]).astype(BF16)
        velocity = velocity + dot_nt(v, owg[b])
    velocity = velocity * jnp.where(cfg == 0, GUIDANCE, 1.0 - GUIDANCE)

    coarse = velocity.astype(BF16)
    fine = (velocity - coarse.astype(F32)).astype(BF16)
    backrow = iota((2 * q, q), 0)
    backcol = iota((2 * q, q), 1)
    backhit = ((backcol >> 2) == (backrow >> 3)) & ((backcol & 3) == (backrow & 3))
    backlow = (backrow & 4) == 0
    put_low = one_hot(backhit & backlow)
    put_high = one_hot(backhit & ~backlow)
    terms = dot(put_low, jnp.concatenate([coarse, fine], axis=1)).reshape(nz, 8, 2 * patch).astype(BF16)
    for b in range(ny):
        v = dot(put_low, lo[b, :, :hb]) + dot(put_high, lo[b, :, hb:])
        back_s[b * nz : (b + 1) * nz, :, :hb] = v.reshape(nz, 8, hb).astype(BF16)
        back_s[b * nz : (b + 1) * nz, :, hb:] = terms

    def back_out(k):
        target, dev = peer(k)
        rcopy(back_s.at[target], back_r.at[n * nz + z], b_s.at[k - 1], b_r.at[k - 1], dev).start()

    times(groups, back_out, 1)
    back_r[n * nz + z] = back_s[n * nz + z]

    column = iota((cap, groups * 8), 1)
    undo = ((column >> 3) * 4 + (column & 3)) == ((iota((cap, groups * 8), 0) + offset) & (cap - 1))
    undo_low = one_hot(undo & ((column & 4) == 0))
    undo_high = one_hot(undo & ((column & 4) != 0))
    index = iota((8, 128), 0) * 128 + iota((8, 128), 1)
    alpha = jnp.where(index == time_ref[0], alpha_ref[...], 0.0)
    alpha = jnp.sum(jnp.sum(alpha, 0, keepdims=True), 1, keepdims=True)
    scaled = jnp.sqrt(alpha) * latent_ref[...]
    factor = jnp.sqrt(1.0 - alpha)
    lanes = iota((1, cap), 1)
    video = (lanes < count) & (lanes + offset >= TEXT)
    times(groups, lambda k: arrived(back_r.at[source(k)], b_r.at[k - 1]), 1)
    v = back_r[:, :, hb:].astype(F32).reshape(groups * 8, 2 * patch).astype(BF16)
    v = dot(undo_low, v).T
    vel_s[...] = v[:patch] + v[patch:]
    rcopy(vel_s, vel_r, c_s.at[0], c_r.at[0], cpart).start()
    v = back_r[:, :, :hb].astype(F32).reshape(groups * 8, hb).astype(BF16)
    out_ref[:, :hb] = dot(undo_low, v).astype(BF16)
    out_ref[:, hb:] = dot(undo_high, v).astype(BF16)

    def slabs_sent(k):
        target = peer(k)[0]
        sent(slab_s.at[target], a_s.at[k - 1])
        sent(back_s.at[target], b_s.at[k - 1])

    times(groups, slabs_sent, 1)
    for k in (1, 2, 3):
        sent(mod_ref, y_s.at[0, k - 1])
        sent(ow_ref, y_s.at[1, k - 1])
    for i in range(2):
        weights_sent(i)
    for i in range(3):
        sent(nst.at[pl.ds(mates[i][2], 2)], e_s.at[i])
        for b in range(2):
            sent(es.at[i, b], f_s.at[i, b])
    for s in range(la):
        for j in range(2):
            sent(xa.at[zmod(z - d * s), mine + j], ag_s.at[s, j])
    for s in range(lb):
        for j in range(2):
            sent(xa.at[zmod(z + d * s), mine + j], ag_s.at[la + s, j])
    for t in range(nz):
        sent(side(zmod(z + d * t), mine), sb_s.at[t])
        for b in range(2):
            sent(sib_s.at[t, b], pr_s.at[t, b])
            if t < nz - 1:
                sent(ring_s.at[t, b], rg_s.at[t, b])
    arrived(vel_r, c_r.at[0])
    clean_ref[...] = jnp.where(video, scaled - factor * (vel_s[...] + vel_r[...]), 0.0)
    sent(vel_s, c_s.at[0])


def on_device(n_wide, n_narrow, hidden, split_table, modulation, w1, w2, ow, latent, timestep):
    cap, bl = hidden.shape[1:]
    ff = w1.shape[1]
    patch = ow.shape[1]
    ny = n_narrow
    nz = n_wide // 4
    q = cap // ny
    gr = n_wide * 2
    sizes = (nz, ny, q, gr, bl, ff, cap, patch)
    groups = ny * nz
    hb = bl // 2
    dma = pltpu.SemaphoreType.DMA
    vm = pltpu.VMEM
    scratch = [
        vm((groups, 8, hb), BF16),
        vm((groups, 8, hb), BF16),
        vm((ny, q, bl), BF16),
        vm((ny, 8, bl), F32),
        vm((ny, patch, bl), BF16),
        vm((ny, bl, ff), BF16),
        vm((ny, ff, bl), BF16),
        vm((ny, q, bl), BF16),
        vm((2, 4 * q, bl), BF16),
        vm((4 * q, gr), F32),
        vm((nz, ny, gr, bl), BF16),
        vm((nz, gr, ff), F32),
        vm((nz, gr, ff), BF16),
        vm((nz, 2, gr, bl), BF16),
        vm((nz, 2, gr, bl), BF16),
        vm((nz - 1, 2, gr, bl), BF16),
        vm((nz - 1, 2, gr, bl), BF16),
        vm((2, gr, bl), BF16),
        vm((3, 2, q, bl), BF16),
        vm((3, 2, q, bl), BF16),
        vm((ny, q, bl), F32),
        vm((ny, q, bl), BF16),
        vm((groups, 8, hb + 2 * patch), BF16),
        vm((groups, 8, hb + 2 * patch), BF16),
        vm((patch, cap), F32),
        vm((patch, cap), F32),
        dma((groups - 1,)),
        dma((groups - 1,)),
        dma((groups - 1,)),
        dma((groups - 1,)),
        dma((2, 3)),
        dma((2, 3)),
        dma((2, 9)),
        dma((2, 9)),
        dma((4,)),
        dma((3,)),
        dma((3,)),
        dma((nz - 1, 2)),
        dma((nz - 1, 2)),
        dma((nz,)),
        dma((nz,)),
        dma((nz, 2)),
        dma((nz, 2)),
        dma((nz - 1, 2)),
        dma((nz - 1, 2)),
        dma((3, 2)),
        dma((3, 2)),
        dma((1,)),
        dma((1,)),
    ]
    hbm = pl.BlockSpec(memory_space=pltpu.HBM)
    smem = pl.BlockSpec(memory_space=pltpu.SMEM)
    vmem = pl.BlockSpec(memory_space=pltpu.VMEM)
    layer_out, clean = pl.pallas_call(
        functools.partial(body, sizes),
        out_shape=(
            jax.ShapeDtypeStruct((cap, bl), BF16),
            jax.ShapeDtypeStruct((patch, cap), F32),
        ),
        in_specs=[smem, smem, vmem, vmem, vmem, hbm, hbm, hbm, hbm],
        out_specs=(vmem, vmem),
        scratch_shapes=scratch,
        compiler_params=pltpu.CompilerParams(
            collective_id=0, has_side_effects=True, vmem_limit_bytes=60 * 1024 * 1024
        ),
    )(
        split_table,
        timestep,
        hidden[0],
        latent.T,
        jnp.asarray(alpha_table()),
        modulation,
        w1,
        w2,
        ow.T,
    )
    return (layer_out[None], clean.T)


def solution(mesh):
    return jax.shard_map(
        functools.partial(on_device, mesh.shape["wide"], mesh.shape["narrow"]),
        mesh=mesh,
        in_specs=(
            P("cfg", "wide", "narrow"),
            P(),
            P(None, "narrow"),
            P("narrow", "wide"),
            P("wide", "narrow"),
            P("narrow", None),
            P("wide", None),
            P(),
        ),
        out_specs=(P("cfg", "wide", "narrow"), P("wide", None)),
        check_vma=False,
    )
```

```python
import functools

import jax
import jax.numpy as jnp
import numpy as np
from jax import lax
from jax.experimental import pallas as pl
from jax.experimental.pallas import tpu as pltpu
from jax.sharding import PartitionSpec as P

TEXT = 226
EPS = 1e-05
GUIDANCE = 6.0
MESH = pl.DeviceIdType.MESH
F32 = jnp.float32
BF16 = jnp.bfloat16
I32 = jnp.int32


def alpha_table():
    start_root = 0.00085**0.5
    end_root = 0.012**0.5
    roots = start_root + (end_root - start_root) * np.arange(1000) / 999.0
    table = np.zeros((8, 128), np.float32)
    table.reshape(-1)[:1000] = np.cumprod(1.0 - roots * roots)
    return table


def dot(a, b):
    return jnp.dot(a, b, preferred_element_type=F32)


def dot_nt(a, b):
    return lax.dot_general(a, b, (((1,), (1,)), ((), ())), preferred_element_type=F32)


def iota(shape, dim):
    return lax.broadcasted_iota(I32, shape, dim)


def one_hot(condition):
    return jnp.where(condition, 1.0, 0.0).astype(BF16)


def body(
    sizes,
    split_ref,
    time_ref,
    hidden_ref,
    latent_ref,
    alpha_ref,
    mod_ref,
    w1_ref,
    w2_ref,
    ow_ref,
    out_ref,
    clean_ref,
    slab_s,
    slab_r,
    xr,
    modg,
    owg,
    w1g,
    w2g,
    nst,
    gx,
    spread,
    xa,
    hid,
    act,
    sib_s,
    sib_r,
    ring_s,
    ring_r,
    tot,
    es,
    er,
    ffb,
    lo,
    back_s,
    back_r,
    vel_s,
    vel_r,
    a_s,
    a_r,
    b_s,
    b_r,
    y_s,
    y_r,
    w_s,
    w_r,
    loc,
    e_s,
    e_r,
    ag_s,
    ag_r,
    sb_s,
    sb_r,
    pr_s,
    pr_r,
    rg_s,
    rg_r,
    f_s,
    f_r,
    c_s,
    c_r,
):
    nz, ny, q, gr, bl, ff, cap, patch = sizes
    feats = ny * bl
    hb = bl // 2
    groups = ny * nz
    la, lb = nz // 2, nz - 1 - nz // 2
    cfg = lax.axis_index("cfg")
    w = lax.axis_index("wide")
    n = lax.axis_index("narrow")
    core = lax.rem(w, 2)
    z = lax.rem(w // 2, nz)
    xh = w // (2 * nz)
    d = 1 - 2 * core

    def wide_of(xh_, z_, core_):
        return xh_ * (2 * nz) + z_ * 2 + core_

    def zmod(v):
        return lax.rem(v + 2 * nz, nz)

    def yid(k):
        return lax.rem(n + k, ny)

    sib = (cfg, wide_of(xh, z, 1 - core), n)
    xpart = (cfg, wide_of(1 - xh, z, core), n)
    diag = (cfg, wide_of(1 - xh, z, 1 - core), n)
    znext = (cfg, wide_of(xh, zmod(z + d), core), n)
    zprev = (cfg, wide_of(xh, zmod(z - d), core), n)
    cpart = (1 - cfg, w, n)

    def ypeer(k):
        return (cfg, w, yid(k))

    def peer(k):
        m = lax.rem(n + k // nz, ny)
        zd = lax.rem(z + lax.rem(k, nz), nz)
        return m * nz + zd, (cfg, wide_of(xh, zd, core), m)

    def source(k):
        m = lax.rem(n + ny - k // nz, ny)
        zd = lax.rem(z + nz - lax.rem(k, nz), nz)
        return m * nz + zd

    def rcopy(src, dst, ssem, rsem, dev):
        return pltpu.make_async_remote_copy(
            src_ref=src, dst_ref=dst, send_sem=ssem, recv_sem=rsem, device_id=dev, device_id_type=MESH
        )

    def arrived(dst, rsem):
        rcopy(dst, dst, rsem, rsem, sib).wait_recv()

    def sent(src, ssem):
        rcopy(src, src, ssem, ssem, sib).wait_send()

    def signal(dev):
        pl.semaphore_signal(barrier, inc=1, device_id=dev, device_id_type=MESH)

    def times(count, action, first=0):
        def step(k, carry):
            action(k)
            return carry

        lax.fori_loop(first, count, step, 0)

    barrier = pltpu.get_barrier_semaphore()
    times(groups, lambda k: signal(peer(k)[1]), 1)
    for dev in (sib, xpart, diag, cpart):
        signal(dev)

    own = [(mod_ref, modg.at[n]), (w1_ref, w1g.at[n]), (w2_ref, w2g.at[n]), (ow_ref, owg.at[n])]
    for i, (src, dst) in enumerate(own):
        pltpu.make_async_copy(src, dst, loc.at[i]).start()

    def rows_of(i, size):
        return pl.ds(pl.multiple_of(i * size, size), size)

    offset = jnp.int32(0)
    count = jnp.int32(0)
    for b in range(split_ref.shape[0]):
        value = split_ref[b]
        offset = offset + jnp.where(b < w, value, 0)
        count = count + jnp.where(b == w, value, 0)
    row = iota((groups * 8, cap), 0)
    residue = (row >> 3) * 4 + (row & 3)
    hit = residue == ((iota((groups * 8, cap), 1) + offset) & (cap - 1))
    low = (row & 4) == 0
    slabs = dot(one_hot(hit & low), hidden_ref[:, :hb]) + dot(one_hot(hit & ~low), hidden_ref[:, hb:])
    slab_s[...] = slabs.reshape(groups, 8, hb).astype(BF16)
    pl.semaphore_wait(barrier, groups - 1 + 4)

    def slab_out(k):
        target, dev = peer(k)
        rcopy(slab_s.at[target], slab_r.at[n * nz + z], a_s.at[k - 1], a_r.at[k - 1], dev).start()

    times(groups, slab_out, 1)
    for k in (1, 3, 2):
        rcopy(mod_ref, modg.at[n], y_s.at[0, k - 1], y_r.at[0, k - 1], ypeer(k)).start()
    slab_r[n * nz + z] = slab_s[n * nz + z]
    weights = [(w1_ref, w1g, bl // 4), (w2_ref, w2g, ff // 4)]
    give, far_own = 3 * cfg, 2 * cfg

    def rows_at(i, first, quarters):
        part = weights[i][2]
        return pl.ds(pl.multiple_of(first * part, part), quarters * part)

    def piece(i, blk, first, quarters):
        return weights[i][1].at[blk, rows_at(i, first, quarters), :]

    sides = ((yid(3), ypeer(1)), (yid(1), ypeer(3)))

    def pass_on(i, blk, first, quarters, sem, dev):
        rcopy(piece(i, blk, first, quarters), piece(i, blk, first, quarters), w_s.at[i, sem], w_r.at[i, sem], dev).start()

    def weight_out(i):
        src = weights[i][0]
        for sem, first, quarters in ((0, give, 1), (2, 1, 2)):
            for k in range(2):
                rcopy(
                    src.at[rows_at(i, first, quarters), :],
                    piece(i, n, first, quarters),
                    w_s.at[i, sem + k],
                    w_r.at[i, sem + k],
                    sides[k][1],
                ).start()

    def weight_give(i):
        for k in range(2):
            arrived(piece(i, sides[k][0], give, 1), w_r.at[i, k])
            pass_on(i, sides[k][0], give, 1, 4 + k, cpart)

    def weight_on(i):
        for k in range(2):
            arrived(piece(i, sides[k][0], 1, 2), w_r.at[i, 2 + k])
            pass_on(i, sides[k][0], far_own + k, 1, 6 + k, sides[k][1])

    def weight_far(i):
        for k in range(2):
            arrived(piece(i, yid(2), far_own + k, 1), w_r.at[i, 6 + k])
        pass_on(i, yid(2), far_own, 2, 8, cpart)

    def weight_near_in(i):
        pltpu.make_async_copy(own[1 + i][0], own[1 + i][1], loc.at[1 + i]).wait()
        for k in range(2):
            arrived(piece(i, sides[k][0], 3 - give, 1), w_r.at[i, 4 + k])

    def weight_far_in(i):
        arrived(piece(i, yid(2), 2 - far_own, 2), w_r.at[i, 8])

    def weights_sent(i):
        for k in range(2):
            sent(weights[i][0].at[rows_at(i, give, 1), :], w_s.at[i, k])
            sent(weights[i][0].at[rows_at(i, 1, 2), :], w_s.at[i, 2 + k])
            sent(piece(i, sides[k][0], give, 1), w_s.at[i, 4 + k])
            sent(piece(i, sides[k][0], far_own + k, 1), w_s.at[i, 6 + k])
        sent(piece(i, yid(2), far_own, 2), w_s.at[i, 8])

    weight_out(0)
    for k in (1, 3, 2):
        rcopy(ow_ref, owg.at[n], y_s.at[1, k - 1], y_r.at[1, k - 1], ypeer(k)).start()
    hid[...] = jnp.zeros_like(hid)

    def slot_table(shape, dim):
        index = iota(shape, dim)
        member = index // q
        inner = index - member * q
        block = (member >> 1) * (2 * nz) + (inner >> 2) * 2 + (member & 1)
        off = jnp.zeros(shape, I32)
        cnt = jnp.zeros(shape, I32)
        for b in range(split_ref.shape[0]):
            value = split_ref[b]
            off = off + jnp.where(block > b, value, 0)
            cnt = cnt + jnp.where(block == b, value, 0)
        lane = inner & 3
        inside = ((n * nz + z) * 4 + lane - off) & (cap - 1)
        position = off + inside
        live = inside < cnt
        spot = jnp.where(live, lane * (gr // 4) + position // cap, -1)
        return live, position, spot

    lane_spot = slot_table((1, 4 * q), 1)[2]
    compact = one_hot(iota((gr, 4 * q), 0) == lane_spot)
    row_live, row_position, row_spot = slot_table((4 * q, 1), 0)
    spread[...] = jnp.where(iota((4 * q, gr), 1) == row_spot, 1.0, 0.0)
    member = xh * 2 + core
    state = jnp.where(row_live, jnp.where(row_position < TEXT, 2, 1), 0)
    tables = jnp.zeros((q, 1), I32)
    for i in range(4):
        tables = tables + jnp.where(member == i, state[i * q : (i + 1) * q], 0)
    live = tables > 0
    text = tables == 2

    def pick(b, row_text, row_video):
        return jnp.where(text, modg[b, pl.ds(row_text, 1), :], modg[b, pl.ds(row_video, 1), :])

    def stats(total, squares):
        average = total / feats
        variance = squares / feats - average * average
        return average, lax.rsqrt(variance + EPS)

    unrow = iota((q, 2 * q), 0)
    uncol = iota((q, 2 * q), 1)
    unhit = ((unrow >> 2) == (uncol >> 3)) & ((unrow & 3) == (uncol & 3))
    unlow = (uncol & 4) == 0
    take_low = one_hot(unhit & unlow)
    take_high = one_hot(unhit & ~unlow)
    weight_give(0)
    times(groups, lambda k: arrived(slab_r.at[source(k)], a_r.at[k - 1]), 1)
    total = jnp.zeros((q, 1), F32)
    squares = jnp.zeros((q, 1), F32)
    for b in range(ny):
        v = slab_r[b * nz : (b + 1) * nz].astype(F32).reshape(nz * 8, hb).astype(BF16)
        for part, take in ((0, take_low), (1, take_high)):
            u = dot(take, v)
            xr[b, :, part * hb : (part + 1) * hb] = u.astype(BF16)
            total = total + jnp.sum(u, -1, keepdims=True)
            squares = squares + jnp.sum(u * u, -1, keepdims=True)
    average, scale = stats(total, squares)
    pltpu.make_async_copy(own[0][0], own[0][1], loc.at[0]).wait()
    for k in (1, 2, 3):
        arrived(modg.at[yid(ny - k)], y_r.at[0, k - 1])
    for b in range(ny):
        v = xr[b].astype(F32)
        nst[b] = ((v - average) * scale * (1.0 + pick(b, 4, 1)) + pick(b, 3, 0)).astype(BF16)

    mine = 2 * core
    other = 2 * (1 - core)
    own_rows = rows_of(member, q)
    mates = [(sib, xh * 2 + 1 - core, other), (xpart, (1 - xh) * 2 + core, mine), (diag, (1 - xh) * 2 + 1 - core, other)]
    for i in (1, 2, 0):
        dev, _, blk = mates[i]
        rcopy(nst.at[pl.ds(blk, 2)], gx.at[:, own_rows, :], e_s.at[i], e_r.at[i], dev).start()
    for j in range(2):
        gx[j, own_rows, :] = nst[mine + j]
    weight_on(0)
    weight_out(1)
    for i in range(3):
        arrived(gx.at[:, rows_of(mates[i][1], q), :], e_r.at[i])
    for j in range(2):
        xa[z, mine + j] = dot(compact, gx[j]).astype(BF16)

    def side(o, first):
        return xa.at[o, pl.ds(first, 2)]

    def relay(o, j, sem, dev):
        rcopy(xa.at[o, mine + j], xa.at[o, mine + j], ag_s.at[sem, j], ag_r.at[sem, j], dev).start()

    def share(u):
        o = zmod(z + d * u)
        rcopy(side(o, mine), side(o, mine), sb_s.at[u % nz], sb_r.at[u % nz], sib).start()

    def work(u):
        o = zmod(z + d * u)
        hid[o] = hid[o] + (dot(xa[o, mine], w1g[mine]) + dot(xa[o, mine + 1], w1g[mine + 1]))
        p = zmod(z - d * u)
        arrived(side(p, other), sb_r.at[zmod(u)])
        hid[p] = hid[p] + (dot(xa[p, other], w1g[other]) + dot(xa[p, other + 1], w1g[other + 1]))

    def gelu(o):
        v = hid[o]
        act[o] = (0.5 * v * (1.0 + jnp.tanh(0.7978845608 * (v + 0.044715 * (v * v * v))))).astype(BF16)

    plan = ((0, weight_far, 0), (1, weight_give, 1), (2, weight_on, 1), (3, weight_far, 1))
    for s in range(la):
        for j in range(2):
            if s > 0:
                arrived(xa.at[zmod(z - d * s), mine + j], ag_r.at[s - 1, j])
            relay(zmod(z - d * s), j, s, znext)
            if 0 < s <= lb:
                arrived(xa.at[zmod(z + d * s), mine + j], ag_r.at[la + s - 1, j])
            if s < lb:
                relay(zmod(z + d * s), j, la + s, zprev)
        share(-s)
        if 0 < s <= lb:
            share(s)
        for at, action, i in plan:
            if s == min(at, la - 1):
                action(i)
        if s == la - 1:
            weight_near_in(0)
            weight_far_in(0)
            work(0)

            def pair(k):
                work(k)
                work(-k)

            times(la, pair, 1)
    for j in range(2):
        arrived(xa.at[zmod(z - d * la), mine + j], ag_r.at[la - 1, j])
    share(-la)
    for s in range(la, lb + 1):
        for j in range(2):
            arrived(xa.at[zmod(z + d * s), mine + j], ag_r.at[la + s - 1, j])
        share(s)
    for u in range(la, nz - la + 1):
        work(u)
    times(nz, gelu)

    far = lax.rem(n + 2, ny)

    def blk_of(side_, b):
        near = side_ == n // 2
        first = jnp.where(near, n, far + 1 - 2 * lax.rem(far, 2))
        second = jnp.where(near, n + 1 - 2 * lax.rem(n, 2), far)
        return first if b == 0 else second

    order = []
    for s in range(la):
        order.append(("next", s, la - s))
        if s < lb:
            order.append(("prev", s, -(lb - s)))
    order.append(("stay", 0, 0))
    slot_of = {(kind, s): t for t, (kind, s, _) in enumerate(order)}

    def sib_part(t, b):
        p = zmod(z - d * order[t][2])
        sib_s[t, b] = dot(act[p], w2g[blk_of(1 - core, b)]).astype(BF16)
        rcopy(sib_s.at[t, b], sib_r.at[t, b], pr_s.at[t, b], pr_r.at[t, b], sib).start()

    def ring_part(t, b):
        kind, s, u = order[t]
        part = dot(act[zmod(z + d * u)], w2g[blk_of(core, b)])
        arrived(sib_r.at[t, b], pr_r.at[t, b])
        part = part + sib_r[t, b].astype(F32)
        if kind == "stay":
            before = [slot_of[("next", la - 1)]] + ([slot_of[("prev", lb - 1)]] if lb else [])
        else:
            before = [slot_of[(kind, s - 1)]] if s else []
        for p in before:
            arrived(ring_r.at[p, b], rg_r.at[p, b])
            part = part + ring_r[p, b].astype(F32)
        if kind == "stay":
            tot[b] = part.astype(BF16)
            for i in range(3):
                dev, index, _ = mates[i]
                es[i, b] = dot(spread[rows_of(index, q), :].astype(BF16), tot[b]).astype(BF16)
                rcopy(es.at[i, b], er.at[i, b], f_s.at[i, b], f_r.at[i, b], dev).start()
            return
        ring_s[t, b] = part.astype(BF16)
        rcopy(
            ring_s.at[t, b], ring_r.at[t, b], rg_s.at[t, b], rg_r.at[t, b], znext if kind == "next" else zprev
        ).start()

    stages = {}
    for t, (kind, s, _) in enumerate(order):
        stages.setdefault(la if kind == "stay" else s, []).append(t)
    lag = 0
    events = []
    for step in range(la + 1 + lag):
        for b in range(2):
            at = step - lag * b
            if 0 <= at <= la:
                events += [(t, b) for t in stages[at]]
    ahead = 2
    weight_near_in(1)
    for t, b in events[:ahead]:
        sib_part(t, b)
    needs_far = False
    for i, (t, b) in enumerate(events):
        if i + ahead < len(events):
            if events[i + ahead][1] == 1 and not needs_far:
                weight_far_in(1)
                needs_far = True
            sib_part(*events[i + ahead])
        ring_part(t, b)

    for b in range(2):
        arrived(er.at[1, b], f_r.at[1, b])
        ffb[blk_of(core, b)] = dot(spread[own_rows, :].astype(BF16), tot[b]) + er[1, b].astype(F32)
    for b in range(2):
        arrived(er.at[0, b], f_r.at[0, b])
        arrived(er.at[2, b], f_r.at[2, b])
        ffb[blk_of(1 - core, b)] = er[0, b].astype(F32) + er[2, b].astype(F32)
    total = jnp.zeros((q, 1), F32)
    squares = jnp.zeros((q, 1), F32)
    for b in range(ny):
        v = xr[b].astype(F32) + pick(b, 5, 2) * ffb[b]
        v = jnp.where(live, v, 0.0).astype(BF16)
        lo[b] = v
        v = v.astype(F32)
        total = total + jnp.sum(v, -1, keepdims=True)
        squares = squares + jnp.sum(v * v, -1, keepdims=True)
    average, scale = stats(total, squares)
    pltpu.make_async_copy(own[3][0], own[3][1], loc.at[3]).wait()
    for k in (1, 2, 3):
        arrived(owg.at[yid(ny - k)], y_r.at[1, k - 1])
    velocity = jnp.zeros((q, patch), F32)
    for b in range(ny):
        v = (lo[b].astype(F32) - average) * scale
        v = (v * (1.0 + modg[b, pl.ds(7, 1), :]) + modg[b, pl.ds(6, 1), :]).astype(BF16)
        velocity = velocity + dot_nt(v, owg[b])
    velocity = velocity * jnp.where(cfg == 0, GUIDANCE, 1.0 - GUIDANCE)

    vel_s[...] = velocity
    rcopy(vel_s, vel_r, c_s.at[0], c_r.at[0], cpart).start()
    backrow = iota((2 * q, q), 0)
    backcol = iota((2 * q, q), 1)
    backhit = ((backcol >> 2) == (backrow >> 3)) & ((backcol & 3) == (backrow & 3))
    backlow = (backrow & 4) == 0
    put_low = one_hot(backhit & backlow)
    put_high = one_hot(backhit & ~backlow)
    for b in range(ny):
        v = dot(put_low, lo[b, :, :hb]) + dot(put_high, lo[b, :, hb:])
        back_s[b * nz : (b + 1) * nz, :, :hb] = v.reshape(nz, 8, hb).astype(BF16)
    arrived(vel_r, c_r.at[0])
    guided = vel_s[...] + vel_r[...]
    coarse = guided.astype(BF16)
    fine = (guided - coarse.astype(F32)).astype(BF16)
    terms = dot(put_low, jnp.concatenate([coarse, fine], axis=1)).reshape(nz, 8, 2 * patch).astype(BF16)
    for b in range(ny):
        back_s[b * nz : (b + 1) * nz, :, hb:] = terms

    def back_out(k):
        target, dev = peer(k)
        rcopy(back_s.at[target], back_r.at[n * nz + z], b_s.at[k - 1], b_r.at[k - 1], dev).start()

    times(groups, back_out, 1)
    back_r[n * nz + z] = back_s[n * nz + z]

    column = iota((cap, groups * 8), 1)
    undo = ((column >> 3) * 4 + (column & 3)) == ((iota((cap, groups * 8), 0) + offset) & (cap - 1))
    undo_low = one_hot(undo & ((column & 4) == 0))
    undo_high = one_hot(undo & ((column & 4) != 0))
    index = iota((8, 128), 0) * 128 + iota((8, 128), 1)
    alpha = jnp.where(index == time_ref[0], alpha_ref[...], 0.0)
    alpha = jnp.sum(jnp.sum(alpha, 0, keepdims=True), 1, keepdims=True)
    scaled = jnp.sqrt(alpha) * latent_ref[...]
    factor = jnp.sqrt(1.0 - alpha)
    lanes = iota((1, cap), 1)
    video = (lanes < count) & (lanes + offset >= TEXT)
    times(groups, lambda k: arrived(back_r.at[source(k)], b_r.at[k - 1]), 1)
    v = back_r[:, :, hb:].astype(F32).reshape(groups * 8, 2 * patch).astype(BF16)
    v = dot(undo_low, v).T
    clean_ref[...] = jnp.where(video, scaled - factor * (v[:patch] + v[patch:]), 0.0)
    v = back_r[:, :, :hb].astype(F32).reshape(groups * 8, hb).astype(BF16)
    out_ref[:, :hb] = dot(undo_low, v).astype(BF16)
    out_ref[:, hb:] = dot(undo_high, v).astype(BF16)

    def slabs_sent(k):
        target = peer(k)[0]
        sent(slab_s.at[target], a_s.at[k - 1])
        sent(back_s.at[target], b_s.at[k - 1])

    times(groups, slabs_sent, 1)
    for k in (1, 2, 3):
        sent(mod_ref, y_s.at[0, k - 1])
        sent(ow_ref, y_s.at[1, k - 1])
    for i in range(2):
        weights_sent(i)
    for i in range(3):
        sent(nst.at[pl.ds(mates[i][2], 2)], e_s.at[i])
        for b in range(2):
            sent(es.at[i, b], f_s.at[i, b])
    for s in range(la):
        for j in range(2):
            sent(xa.at[zmod(z - d * s), mine + j], ag_s.at[s, j])
    for s in range(lb):
        for j in range(2):
            sent(xa.at[zmod(z + d * s), mine + j], ag_s.at[la + s, j])
    for t in range(nz):
        sent(side(zmod(z + d * t), mine), sb_s.at[t])
        for b in range(2):
            sent(sib_s.at[t, b], pr_s.at[t, b])
            if t < nz - 1:
                sent(ring_s.at[t, b], rg_s.at[t, b])
    sent(vel_s, c_s.at[0])


def on_device(n_wide, n_narrow, hidden, split_table, modulation, w1, w2, ow, latent, timestep):
    cap, bl = hidden.shape[1:]
    ff = w1.shape[1]
    patch = ow.shape[1]
    ny = n_narrow
    nz = n_wide // 4
    q = cap // ny
    gr = n_wide * 2
    sizes = (nz, ny, q, gr, bl, ff, cap, patch)
    groups = ny * nz
    hb = bl // 2
    dma = pltpu.SemaphoreType.DMA
    vm = pltpu.VMEM
    scratch = [
        vm((groups, 8, hb), BF16),
        vm((groups, 8, hb), BF16),
        vm((ny, q, bl), BF16),
        vm((ny, 8, bl), F32),
        vm((ny, patch, bl), BF16),
        vm((ny, bl, ff), BF16),
        vm((ny, ff, bl), BF16),
        vm((ny, q, bl), BF16),
        vm((2, 4 * q, bl), BF16),
        vm((4 * q, gr), F32),
        vm((nz, ny, gr, bl), BF16),
        vm((nz, gr, ff), F32),
        vm((nz, gr, ff), BF16),
        vm((nz, 2, gr, bl), BF16),
        vm((nz, 2, gr, bl), BF16),
        vm((nz - 1, 2, gr, bl), BF16),
        vm((nz - 1, 2, gr, bl), BF16),
        vm((2, gr, bl), BF16),
        vm((3, 2, q, bl), BF16),
        vm((3, 2, q, bl), BF16),
        vm((ny, q, bl), F32),
        vm((ny, q, bl), BF16),
        vm((groups, 8, hb + 2 * patch), BF16),
        vm((groups, 8, hb + 2 * patch), BF16),
        vm((q, patch), F32),
        vm((q, patch), F32),
        dma((groups - 1,)),
        dma((groups - 1,)),
        dma((groups - 1,)),
        dma((groups - 1,)),
        dma((2, 3)),
        dma((2, 3)),
        dma((2, 9)),
        dma((2, 9)),
        dma((4,)),
        dma((3,)),
        dma((3,)),
        dma((nz - 1, 2)),
        dma((nz - 1, 2)),
        dma((nz,)),
        dma((nz,)),
        dma((nz, 2)),
        dma((nz, 2)),
        dma((nz - 1, 2)),
        dma((nz - 1, 2)),
        dma((3, 2)),
        dma((3, 2)),
        dma((1,)),
        dma((1,)),
    ]
    hbm = pl.BlockSpec(memory_space=pltpu.HBM)
    smem = pl.BlockSpec(memory_space=pltpu.SMEM)
    vmem = pl.BlockSpec(memory_space=pltpu.VMEM)
    layer_out, clean = pl.pallas_call(
        functools.partial(body, sizes),
        out_shape=(
            jax.ShapeDtypeStruct((cap, bl), BF16),
            jax.ShapeDtypeStruct((patch, cap), F32),
        ),
        in_specs=[smem, smem, vmem, vmem, vmem, hbm, hbm, hbm, hbm],
        out_specs=(vmem, vmem),
        scratch_shapes=scratch,
        compiler_params=pltpu.CompilerParams(
            collective_id=0, has_side_effects=True, vmem_limit_bytes=60 * 1024 * 1024
        ),
    )(
        split_table,
        timestep,
        hidden[0],
        latent.T,
        jnp.asarray(alpha_table()),
        modulation,
        w1,
        w2,
        ow.T,
    )
    return (layer_out[None], clean.T)


def solution(mesh):
    return jax.shard_map(
        functools.partial(on_device, mesh.shape["wide"], mesh.shape["narrow"]),
        mesh=mesh,
        in_specs=(
            P("cfg", "wide", "narrow"),
            P(),
            P(None, "narrow"),
            P("narrow", "wide"),
            P("wide", "narrow"),
            P("narrow", None),
            P("wide", None),
            P(),
        ),
        out_specs=(P("cfg", "wide", "narrow"), P("wide", None)),
        check_vma=False,
    )
```

```python
import functools

import jax
import jax.numpy as jnp
import numpy as np
from jax import lax
from jax.experimental import pallas as pl
from jax.experimental.pallas import tpu as pltpu
from jax.sharding import PartitionSpec as P

TEXT = 226
EPS = 1e-05
GUIDANCE = 6.0
MESH = pl.DeviceIdType.MESH
F32 = jnp.float32
BF16 = jnp.bfloat16
I32 = jnp.int32


def alpha_table():
    start_root = 0.00085**0.5
    end_root = 0.012**0.5
    roots = start_root + (end_root - start_root) * np.arange(1000) / 999.0
    table = np.zeros((8, 128), np.float32)
    table.reshape(-1)[:1000] = np.cumprod(1.0 - roots * roots)
    return table


def dot(a, b):
    return jnp.dot(a, b, preferred_element_type=F32)


def dot_nt(a, b):
    return lax.dot_general(a, b, (((1,), (1,)), ((), ())), preferred_element_type=F32)


def iota(shape, dim):
    return lax.broadcasted_iota(I32, shape, dim)


def one_hot(condition):
    return jnp.where(condition, 1.0, 0.0).astype(BF16)


def body(
    sizes,
    split_ref,
    time_ref,
    hidden_ref,
    latent_ref,
    alpha_ref,
    mod_ref,
    w1_ref,
    w2_ref,
    ow_ref,
    out_ref,
    clean_ref,
    slab_s,
    slab_r,
    xr,
    modg,
    owg,
    w1g,
    w2g,
    nst,
    gx,
    spread,
    xa,
    hid,
    act,
    sib_s,
    sib_r,
    ring_s,
    ring_r,
    tot,
    es,
    er,
    ffb,
    lo,
    back_s,
    back_r,
    vel_s,
    vel_r,
    a_s,
    a_r,
    b_s,
    b_r,
    y_s,
    y_r,
    w_s,
    w_r,
    loc,
    e_s,
    e_r,
    ag_s,
    ag_r,
    sb_s,
    sb_r,
    pr_s,
    pr_r,
    rg_s,
    rg_r,
    f_s,
    f_r,
    c_s,
    c_r,
):
    nz, ny, q, gr, bl, ff, cap, patch = sizes
    feats = ny * bl
    hb = bl // 2
    groups = ny * nz
    la, lb = nz // 2, nz - 1 - nz // 2
    cfg = lax.axis_index("cfg")
    w = lax.axis_index("wide")
    n = lax.axis_index("narrow")
    core = lax.rem(w, 2)
    z = lax.rem(w // 2, nz)
    xh = w // (2 * nz)
    d = 1 - 2 * core

    def wide_of(xh_, z_, core_):
        return xh_ * (2 * nz) + z_ * 2 + core_

    def zmod(v):
        return lax.rem(v + 2 * nz, nz)

    def yid(k):
        return lax.rem(n + k, ny)

    sib = (cfg, wide_of(xh, z, 1 - core), n)
    xpart = (cfg, wide_of(1 - xh, z, core), n)
    diag = (cfg, wide_of(1 - xh, z, 1 - core), n)
    znext = (cfg, wide_of(xh, zmod(z + d), core), n)
    zprev = (cfg, wide_of(xh, zmod(z - d), core), n)
    cpart = (1 - cfg, w, n)

    def ypeer(k):
        return (cfg, w, yid(k))

    def peer(k):
        m = lax.rem(n + k // nz, ny)
        zd = lax.rem(z + lax.rem(k, nz), nz)
        return m * nz + zd, (cfg, wide_of(xh, zd, core), m)

    def source(k):
        m = lax.rem(n + ny - k // nz, ny)
        zd = lax.rem(z + nz - lax.rem(k, nz), nz)
        return m * nz + zd

    def rcopy(src, dst, ssem, rsem, dev):
        return pltpu.make_async_remote_copy(
            src_ref=src, dst_ref=dst, send_sem=ssem, recv_sem=rsem, device_id=dev, device_id_type=MESH
        )

    def arrived(dst, rsem):
        rcopy(dst, dst, rsem, rsem, sib).wait_recv()

    def sent(src, ssem):
        rcopy(src, src, ssem, ssem, sib).wait_send()

    def signal(dev):
        pl.semaphore_signal(barrier, inc=1, device_id=dev, device_id_type=MESH)

    def times(count, action, first=0):
        def step(k, carry):
            action(k)
            return carry

        lax.fori_loop(first, count, step, 0)

    barrier = pltpu.get_barrier_semaphore()
    times(groups, lambda k: signal(peer(k)[1]), 1)
    for dev in (sib, xpart, diag, cpart):
        signal(dev)

    own = [(mod_ref, modg.at[n]), (w1_ref, w1g.at[n]), (w2_ref, w2g.at[n]), (ow_ref, owg.at[n])]
    for i, (src, dst) in enumerate(own):
        pltpu.make_async_copy(src, dst, loc.at[i]).start()

    def rows_of(i, size):
        return pl.ds(pl.multiple_of(i * size, size), size)

    offset = jnp.int32(0)
    count = jnp.int32(0)
    for b in range(split_ref.shape[0]):
        value = split_ref[b]
        offset = offset + jnp.where(b < w, value, 0)
        count = count + jnp.where(b == w, value, 0)
    row = iota((groups * 8, cap), 0)
    residue = (row >> 3) * 4 + (row & 3)
    hit = residue == ((iota((groups * 8, cap), 1) + offset) & (cap - 1))
    low = (row & 4) == 0
    slabs = dot(one_hot(hit & low), hidden_ref[:, :hb]) + dot(one_hot(hit & ~low), hidden_ref[:, hb:])
    slab_s[...] = slabs.reshape(groups, 8, hb).astype(BF16)
    pl.semaphore_wait(barrier, groups - 1 + 4)

    def slab_out(k):
        target, dev = peer(k)
        rcopy(slab_s.at[target], slab_r.at[n * nz + z], a_s.at[k - 1], a_r.at[k - 1], dev).start()

    times(groups, slab_out, 1)
    for k in (1, 3, 2):
        rcopy(mod_ref, modg.at[n], y_s.at[0, k - 1], y_r.at[0, k - 1], ypeer(k)).start()
    slab_r[n * nz + z] = slab_s[n * nz + z]
    weights = [(w1_ref, w1g, bl // 4), (w2_ref, w2g, ff // 4)]
    give, far_own = 3 * cfg, 2 * cfg

    def rows_at(i, first, quarters):
        part = weights[i][2]
        return pl.ds(pl.multiple_of(first * part, part), quarters * part)

    def piece(i, blk, first, quarters):
        return weights[i][1].at[blk, rows_at(i, first, quarters), :]

    sides = ((yid(3), ypeer(1)), (yid(1), ypeer(3)))

    def pass_on(i, blk, first, quarters, sem, dev):
        rcopy(piece(i, blk, first, quarters), piece(i, blk, first, quarters), w_s.at[i, sem], w_r.at[i, sem], dev).start()

    def weight_out(i):
        src = weights[i][0]
        for sem, first, quarters in ((0, give, 1), (2, 1, 2)):
            for k in range(2):
                rcopy(
                    src.at[rows_at(i, first, quarters), :],
                    piece(i, n, first, quarters),
                    w_s.at[i, sem + k],
                    w_r.at[i, sem + k],
                    sides[k][1],
                ).start()

    def weight_give(i):
        for k in range(2):
            arrived(piece(i, sides[k][0], give, 1), w_r.at[i, k])
            pass_on(i, sides[k][0], give, 1, 4 + k, cpart)

    def weight_on(i):
        for k in range(2):
            arrived(piece(i, sides[k][0], 1, 2), w_r.at[i, 2 + k])
            pass_on(i, sides[k][0], far_own + k, 1, 6 + k, sides[k][1])

    def weight_far(i):
        for k in range(2):
            arrived(piece(i, yid(2), far_own + k, 1), w_r.at[i, 6 + k])
        pass_on(i, yid(2), far_own, 2, 8, cpart)

    def weight_near_in(i):
        pltpu.make_async_copy(own[1 + i][0], own[1 + i][1], loc.at[1 + i]).wait()
        for k in range(2):
            arrived(piece(i, sides[k][0], 3 - give, 1), w_r.at[i, 4 + k])

    def weight_far_in(i):
        arrived(piece(i, yid(2), 2 - far_own, 2), w_r.at[i, 8])

    def weights_sent(i):
        for k in range(2):
            sent(weights[i][0].at[rows_at(i, give, 1), :], w_s.at[i, k])
            sent(weights[i][0].at[rows_at(i, 1, 2), :], w_s.at[i, 2 + k])
            sent(piece(i, sides[k][0], give, 1), w_s.at[i, 4 + k])
            sent(piece(i, sides[k][0], far_own + k, 1), w_s.at[i, 6 + k])
        sent(piece(i, yid(2), far_own, 2), w_s.at[i, 8])

    weight_out(0)
    for k in (1, 3, 2):
        rcopy(ow_ref, owg.at[n], y_s.at[1, k - 1], y_r.at[1, k - 1], ypeer(k)).start()
    hid[...] = jnp.zeros_like(hid)

    def slot_table(shape, dim):
        index = iota(shape, dim)
        member = index // q
        inner = index - member * q
        block = (member >> 1) * (2 * nz) + (inner >> 2) * 2 + (member & 1)
        off = jnp.zeros(shape, I32)
        cnt = jnp.zeros(shape, I32)
        for b in range(split_ref.shape[0]):
            value = split_ref[b]
            off = off + jnp.where(block > b, value, 0)
            cnt = cnt + jnp.where(block == b, value, 0)
        lane = inner & 3
        inside = ((n * nz + z) * 4 + lane - off) & (cap - 1)
        position = off + inside
        live = inside < cnt
        spot = jnp.where(live, lane * (gr // 4) + position // cap, -1)
        return live, position, spot

    lane_spot = slot_table((1, 4 * q), 1)[2]
    compact = one_hot(iota((gr, 4 * q), 0) == lane_spot)
    row_live, row_position, row_spot = slot_table((4 * q, 1), 0)
    spread[...] = jnp.where(iota((4 * q, gr), 1) == row_spot, 1.0, 0.0)
    member = xh * 2 + core
    state = jnp.where(row_live, jnp.where(row_position < TEXT, 2, 1), 0)
    tables = jnp.zeros((q, 1), I32)
    for i in range(4):
        tables = tables + jnp.where(member == i, state[i * q : (i + 1) * q], 0)
    live = tables > 0
    text = tables == 2

    def pick(b, row_text, row_video):
        return jnp.where(text, modg[b, pl.ds(row_text, 1), :], modg[b, pl.ds(row_video, 1), :])

    def stats(total, squares):
        average = total / feats
        variance = squares / feats - average * average
        return average, lax.rsqrt(variance + EPS)

    unrow = iota((q, 2 * q), 0)
    uncol = iota((q, 2 * q), 1)
    unhit = ((unrow >> 2) == (uncol >> 3)) & ((unrow & 3) == (uncol & 3))
    unlow = (uncol & 4) == 0
    take_low = one_hot(unhit & unlow)
    take_high = one_hot(unhit & ~unlow)
    weight_give(0)
    times(groups, lambda k: arrived(slab_r.at[source(k)], a_r.at[k - 1]), 1)
    weight_out(1)
    total = jnp.zeros((q, 1), F32)
    squares = jnp.zeros((q, 1), F32)
    for b in range(ny):
        v = slab_r[b * nz : (b + 1) * nz].astype(F32).reshape(nz * 8, hb).astype(BF16)
        for part, take in ((0, take_low), (1, take_high)):
            u = dot(take, v)
            xr[b, :, part * hb : (part + 1) * hb] = u.astype(BF16)
            total = total + jnp.sum(u, -1, keepdims=True)
            squares = squares + jnp.sum(u * u, -1, keepdims=True)
    average, scale = stats(total, squares)
    pltpu.make_async_copy(own[0][0], own[0][1], loc.at[0]).wait()
    for k in (1, 2, 3):
        arrived(modg.at[yid(ny - k)], y_r.at[0, k - 1])
    for b in range(ny):
        v = xr[b].astype(F32)
        nst[b] = ((v - average) * scale * (1.0 + pick(b, 4, 1)) + pick(b, 3, 0)).astype(BF16)

    mine = 2 * core
    other = 2 * (1 - core)
    own_rows = rows_of(member, q)
    mates = [(sib, xh * 2 + 1 - core, other), (xpart, (1 - xh) * 2 + core, mine), (diag, (1 - xh) * 2 + 1 - core, other)]
    for i in (1, 2, 0):
        dev, _, blk = mates[i]
        rcopy(nst.at[pl.ds(blk, 2)], gx.at[:, own_rows, :], e_s.at[i], e_r.at[i], dev).start()
    for j in range(2):
        gx[j, own_rows, :] = nst[mine + j]
    weight_on(0)
    for i in range(3):
        arrived(gx.at[:, rows_of(mates[i][1], q), :], e_r.at[i])
    for j in range(2):
        xa[z, mine + j] = dot(compact, gx[j]).astype(BF16)

    def side(o, first):
        return xa.at[o, pl.ds(first, 2)]

    def relay(o, j, sem, dev):
        rcopy(xa.at[o, mine + j], xa.at[o, mine + j], ag_s.at[sem, j], ag_r.at[sem, j], dev).start()

    def share(u):
        o = zmod(z + d * u)
        rcopy(side(o, mine), side(o, mine), sb_s.at[u % nz], sb_r.at[u % nz], sib).start()

    def work(u):
        o = zmod(z + d * u)
        hid[o] = hid[o] + (dot(xa[o, mine], w1g[mine]) + dot(xa[o, mine + 1], w1g[mine + 1]))
        p = zmod(z - d * u)
        arrived(side(p, other), sb_r.at[zmod(u)])
        hid[p] = hid[p] + (dot(xa[p, other], w1g[other]) + dot(xa[p, other + 1], w1g[other + 1]))

    def gelu(o):
        v = hid[o]
        act[o] = (0.5 * v * (1.0 + jnp.tanh(0.7978845608 * (v + 0.044715 * (v * v * v))))).astype(BF16)

    plan = ((0, weight_far, 0), (1, weight_give, 1), (2, weight_on, 1), (3, weight_far, 1))
    for s in range(la):
        for j in range(2):
            if s > 0:
                arrived(xa.at[zmod(z - d * s), mine + j], ag_r.at[s - 1, j])
            relay(zmod(z - d * s), j, s, znext)
            if 0 < s <= lb:
                arrived(xa.at[zmod(z + d * s), mine + j], ag_r.at[la + s - 1, j])
            if s < lb:
                relay(zmod(z + d * s), j, la + s, zprev)
        share(-s)
        if 0 < s <= lb:
            share(s)
        for at, action, i in plan:
            if s == min(at, la - 1):
                action(i)
        if s == la - 1:
            weight_near_in(0)
            weight_far_in(0)
            work(0)

            def pair(k):
                work(k)
                work(-k)

            times(la, pair, 1)
    for j in range(2):
        arrived(xa.at[zmod(z - d * la), mine + j], ag_r.at[la - 1, j])
    share(-la)
    for s in range(la, lb + 1):
        for j in range(2):
            arrived(xa.at[zmod(z + d * s), mine + j], ag_r.at[la + s - 1, j])
        share(s)
    for u in range(la, nz - la + 1):
        work(u)
    times(nz, gelu)

    far = lax.rem(n + 2, ny)

    def blk_of(side_, b):
        near = side_ == n // 2
        first = jnp.where(near, n, far + 1 - 2 * lax.rem(far, 2))
        second = jnp.where(near, n + 1 - 2 * lax.rem(n, 2), far)
        return first if b == 0 else second

    order = []
    for s in range(la):
        order.append(("next", s, la - s))
        if s < lb:
            order.append(("prev", s, -(lb - s)))
    order.append(("stay", 0, 0))
    slot_of = {(kind, s): t for t, (kind, s, _) in enumerate(order)}

    def sib_part(t, b):
        p = zmod(z - d * order[t][2])
        sib_s[t, b] = dot(act[p], w2g[blk_of(1 - core, b)]).astype(BF16)
        rcopy(sib_s.at[t, b], sib_r.at[t, b], pr_s.at[t, b], pr_r.at[t, b], sib).start()

    def ring_part(t, b):
        kind, s, u = order[t]
        part = dot(act[zmod(z + d * u)], w2g[blk_of(core, b)])
        arrived(sib_r.at[t, b], pr_r.at[t, b])
        part = part + sib_r[t, b].astype(F32)
        if kind == "stay":
            before = [slot_of[("next", la - 1)]] + ([slot_of[("prev", lb - 1)]] if lb else [])
        else:
            before = [slot_of[(kind, s - 1)]] if s else []
        for p in before:
            arrived(ring_r.at[p, b], rg_r.at[p, b])
            part = part + ring_r[p, b].astype(F32)
        if kind == "stay":
            tot[b] = part.astype(BF16)
            for i in range(3):
                dev, index, _ = mates[i]
                es[i, b] = dot(spread[rows_of(index, q), :].astype(BF16), tot[b]).astype(BF16)
                rcopy(es.at[i, b], er.at[i, b], f_s.at[i, b], f_r.at[i, b], dev).start()
            return
        ring_s[t, b] = part.astype(BF16)
        rcopy(
            ring_s.at[t, b], ring_r.at[t, b], rg_s.at[t, b], rg_r.at[t, b], znext if kind == "next" else zprev
        ).start()

    stages = {}
    for t, (kind, s, _) in enumerate(order):
        stages.setdefault(la if kind == "stay" else s, []).append(t)
    lag = 0
    events = []
    for step in range(la + 1 + lag):
        for b in range(2):
            at = step - lag * b
            if 0 <= at <= la:
                events += [(t, b) for t in stages[at]]
    ahead = 2
    weight_near_in(1)
    for t, b in events[:ahead]:
        sib_part(t, b)
    needs_far = False
    for i, (t, b) in enumerate(events):
        if i + ahead < len(events):
            if events[i + ahead][1] == 1 and not needs_far:
                weight_far_in(1)
                needs_far = True
            sib_part(*events[i + ahead])
        ring_part(t, b)

    for b in range(2):
        arrived(er.at[1, b], f_r.at[1, b])
        ffb[blk_of(core, b)] = dot(spread[own_rows, :].astype(BF16), tot[b]) + er[1, b].astype(F32)
    for b in range(2):
        arrived(er.at[0, b], f_r.at[0, b])
        arrived(er.at[2, b], f_r.at[2, b])
        ffb[blk_of(1 - core, b)] = er[0, b].astype(F32) + er[2, b].astype(F32)
    total = jnp.zeros((q, 1), F32)
    squares = jnp.zeros((q, 1), F32)
    for b in range(ny):
        v = xr[b].astype(F32) + pick(b, 5, 2) * ffb[b]
        v = jnp.where(live, v, 0.0).astype(BF16)
        lo[b] = v
        v = v.astype(F32)
        total = total + jnp.sum(v, -1, keepdims=True)
        squares = squares + jnp.sum(v * v, -1, keepdims=True)
    average, scale = stats(total, squares)
    pltpu.make_async_copy(own[3][0], own[3][1], loc.at[3]).wait()
    for k in (1, 2, 3):
        arrived(owg.at[yid(ny - k)], y_r.at[1, k - 1])
    velocity = jnp.zeros((q, patch), F32)
    for b in range(ny):
        v = (lo[b].astype(F32) - average) * scale
        v = (v * (1.0 + modg[b, pl.ds(7, 1), :]) + modg[b, pl.ds(6, 1), :]).astype(BF16)
        velocity = velocity + dot_nt(v, owg[b])
    velocity = velocity * jnp.where(cfg == 0, GUIDANCE, 1.0 - GUIDANCE)

    vel_s[...] = velocity
    rcopy(vel_s, vel_r, c_s.at[0], c_r.at[0], cpart).start()
    backrow = iota((2 * q, q), 0)
    backcol = iota((2 * q, q), 1)
    backhit = ((backcol >> 2) == (backrow >> 3)) & ((backcol & 3) == (backrow & 3))
    backlow = (backrow & 4) == 0
    put_low = one_hot(backhit & backlow)
    put_high = one_hot(backhit & ~backlow)
    for b in range(ny):
        v = dot(put_low, lo[b, :, :hb]) + dot(put_high, lo[b, :, hb:])
        back_s[b * nz : (b + 1) * nz, :, :hb] = v.reshape(nz, 8, hb).astype(BF16)
    arrived(vel_r, c_r.at[0])
    guided = vel_s[...] + vel_r[...]
    coarse = guided.astype(BF16)
    fine = (guided - coarse.astype(F32)).astype(BF16)
    terms = dot(put_low, jnp.concatenate([coarse, fine], axis=1)).reshape(nz, 8, 2 * patch).astype(BF16)
    for b in range(ny):
        back_s[b * nz : (b + 1) * nz, :, hb:] = terms

    def back_out(k):
        target, dev = peer(k)
        rcopy(back_s.at[target], back_r.at[n * nz + z], b_s.at[k - 1], b_r.at[k - 1], dev).start()

    times(groups, back_out, 1)
    back_r[n * nz + z] = back_s[n * nz + z]

    column = iota((cap, groups * 8), 1)
    undo = ((column >> 3) * 4 + (column & 3)) == ((iota((cap, groups * 8), 0) + offset) & (cap - 1))
    undo_low = one_hot(undo & ((column & 4) == 0))
    undo_high = one_hot(undo & ((column & 4) != 0))
    index = iota((8, 128), 0) * 128 + iota((8, 128), 1)
    alpha = jnp.where(index == time_ref[0], alpha_ref[...], 0.0)
    alpha = jnp.sum(jnp.sum(alpha, 0, keepdims=True), 1, keepdims=True)
    scaled = jnp.sqrt(alpha) * latent_ref[...]
    factor = jnp.sqrt(1.0 - alpha)
    lanes = iota((1, cap), 1)
    video = (lanes < count) & (lanes + offset >= TEXT)
    times(groups, lambda k: arrived(back_r.at[source(k)], b_r.at[k - 1]), 1)
    v = back_r[:, :, hb:].astype(F32).reshape(groups * 8, 2 * patch).astype(BF16)
    v = dot(undo_low, v).T
    clean_ref[...] = jnp.where(video, scaled - factor * (v[:patch] + v[patch:]), 0.0)
    v = back_r[:, :, :hb].astype(F32).reshape(groups * 8, hb).astype(BF16)
    out_ref[:, :hb] = dot(undo_low, v).astype(BF16)
    out_ref[:, hb:] = dot(undo_high, v).astype(BF16)

    def slabs_sent(k):
        target = peer(k)[0]
        sent(slab_s.at[target], a_s.at[k - 1])
        sent(back_s.at[target], b_s.at[k - 1])

    times(groups, slabs_sent, 1)
    for k in (1, 2, 3):
        sent(mod_ref, y_s.at[0, k - 1])
        sent(ow_ref, y_s.at[1, k - 1])
    for i in range(2):
        weights_sent(i)
    for i in range(3):
        sent(nst.at[pl.ds(mates[i][2], 2)], e_s.at[i])
        for b in range(2):
            sent(es.at[i, b], f_s.at[i, b])
    for s in range(la):
        for j in range(2):
            sent(xa.at[zmod(z - d * s), mine + j], ag_s.at[s, j])
    for s in range(lb):
        for j in range(2):
            sent(xa.at[zmod(z + d * s), mine + j], ag_s.at[la + s, j])
    for t in range(nz):
        sent(side(zmod(z + d * t), mine), sb_s.at[t])
        for b in range(2):
            sent(sib_s.at[t, b], pr_s.at[t, b])
            if t < nz - 1:
                sent(ring_s.at[t, b], rg_s.at[t, b])
    sent(vel_s, c_s.at[0])


def on_device(n_wide, n_narrow, hidden, split_table, modulation, w1, w2, ow, latent, timestep):
    cap, bl = hidden.shape[1:]
    ff = w1.shape[1]
    patch = ow.shape[1]
    ny = n_narrow
    nz = n_wide // 4
    q = cap // ny
    gr = n_wide * 2
    sizes = (nz, ny, q, gr, bl, ff, cap, patch)
    groups = ny * nz
    hb = bl // 2
    dma = pltpu.SemaphoreType.DMA
    vm = pltpu.VMEM
    scratch = [
        vm((groups, 8, hb), BF16),
        vm((groups, 8, hb), BF16),
        vm((ny, q, bl), BF16),
        vm((ny, 8, bl), F32),
        vm((ny, patch, bl), BF16),
        vm((ny, bl, ff), BF16),
        vm((ny, ff, bl), BF16),
        vm((ny, q, bl), BF16),
        vm((2, 4 * q, bl), BF16),
        vm((4 * q, gr), F32),
        vm((nz, ny, gr, bl), BF16),
        vm((nz, gr, ff), F32),
        vm((nz, gr, ff), BF16),
        vm((nz, 2, gr, bl), BF16),
        vm((nz, 2, gr, bl), BF16),
        vm((nz - 1, 2, gr, bl), BF16),
        vm((nz - 1, 2, gr, bl), BF16),
        vm((2, gr, bl), BF16),
        vm((3, 2, q, bl), BF16),
        vm((3, 2, q, bl), BF16),
        vm((ny, q, bl), F32),
        vm((ny, q, bl), BF16),
        vm((groups, 8, hb + 2 * patch), BF16),
        vm((groups, 8, hb + 2 * patch), BF16),
        vm((q, patch), F32),
        vm((q, patch), F32),
        dma((groups - 1,)),
        dma((groups - 1,)),
        dma((groups - 1,)),
        dma((groups - 1,)),
        dma((2, 3)),
        dma((2, 3)),
        dma((2, 9)),
        dma((2, 9)),
        dma((4,)),
        dma((3,)),
        dma((3,)),
        dma((nz - 1, 2)),
        dma((nz - 1, 2)),
        dma((nz,)),
        dma((nz,)),
        dma((nz, 2)),
        dma((nz, 2)),
        dma((nz - 1, 2)),
        dma((nz - 1, 2)),
        dma((3, 2)),
        dma((3, 2)),
        dma((1,)),
        dma((1,)),
    ]
    hbm = pl.BlockSpec(memory_space=pltpu.HBM)
    smem = pl.BlockSpec(memory_space=pltpu.SMEM)
    vmem = pl.BlockSpec(memory_space=pltpu.VMEM)
    layer_out, clean = pl.pallas_call(
        functools.partial(body, sizes),
        out_shape=(
            jax.ShapeDtypeStruct((cap, bl), BF16),
            jax.ShapeDtypeStruct((patch, cap), F32),
        ),
        in_specs=[smem, smem, vmem, vmem, vmem, hbm, hbm, hbm, hbm],
        out_specs=(vmem, vmem),
        scratch_shapes=scratch,
        compiler_params=pltpu.CompilerParams(
            collective_id=0, has_side_effects=True, vmem_limit_bytes=60 * 1024 * 1024
        ),
    )(
        split_table,
        timestep,
        hidden[0],
        latent.T,
        jnp.asarray(alpha_table()),
        modulation,
        w1,
        w2,
        ow.T,
    )
    return (layer_out[None], clean.T)


def solution(mesh):
    return jax.shard_map(
        functools.partial(on_device, mesh.shape["wide"], mesh.shape["narrow"]),
        mesh=mesh,
        in_specs=(
            P("cfg", "wide", "narrow"),
            P(),
            P(None, "narrow"),
            P("narrow", "wide"),
            P("wide", "narrow"),
            P("narrow", None),
            P("wide", None),
            P(),
        ),
        out_specs=(P("cfg", "wide", "narrow"), P("wide", None)),
        check_vma=False,
    )
```
